256 devices in a mesh: lat: 8 (over y, x_hi), lon: 32 (over z, x_lo, core).
Axes of the slice: x: 4 (x_hi: 2, x_lo: 2; x = x_hi * 2 + x_lo), y: 4, z: 8, core: 2. Of those that a mesh axis runs over, the one named last changes fastest.
Arguments:
- features: bfloat16 [256, 4096, 128], P('lat', 'lon'), may hold values from -6 to 6
- land_mask: int32 [256, 4096], P('lat', 'lon'), may hold values 0 or 1
- dw_weight: float32 [7, 7, 128], replicated, may hold values from -0.875 to 0.875
- dw_bias: float32 [128], replicated, may hold values from -3 to 3
- norm_gain: float32 [128], replicated, may hold values from 0.25 to 1.75
- norm_shift: float32 [128], replicated, may hold values from -3 to 3
- expand_weight: bfloat16 [128, 512], replicated, may hold values from -0.5 to 0.5
- expand_bias: float32 [512], replicated, may hold values from -3 to 3
- project_weight: bfloat16 [512, 128], replicated, may hold values from -0.25 to 0.25
- project_bias: float32 [128], replicated, may hold values from -3 to 3
- layer_scale: float32 [128], replicated, may hold values from 0.3 to 1
- out_gain: float32 [128], replicated, may hold values from 0.25 to 1.75
- out_shift: float32 [128], replicated, may hold values from -3 to 3
- coarse_weight: bfloat16 [4, 4, 128, 256], replicated, may hold values from -0.125 to 0.125
- coarse_bias: float32 [256], replicated, may hold values from -3 to 3
Outputs:
- coarse: bfloat16 [128, 2048, 256], P('lat', 'lon')
The draws below stay inside these ranges and needn't reach their ends.
All inputs are finite; a program needn't handle non-finite values. No bound on the sum of `land_mask` on one device may be relied on, other than what follows from the above.
Results may differ from the reference program's by a relative error of at most 0.0051.
Values may be sent and summed in bfloat16 or wider, within the bound.
No kernel may reach another device: no remote copies, remote signals or barrier semaphores. Data moves between devices by JAX's collectives and lax.ppermute only.
A program may use at most 64 MiB of HBM per device.

```python
import math
import jax
import jax.numpy as jnp
from jax import lax

C = 128
HID = 512
OUT = 256
KS = 7
CY = 32
NY = 256
NX = 4096
N_LAT = 8


def set_ends(drawn, own_key, smallest, top_value):
    dims = drawn.shape
    place = [jax.random.randint(jax.random.fold_in(own_key, axis), (), 0, dims[axis]) for axis in range(len(dims))]
    drawn = drawn.at[tuple(place)].set(smallest)
    longest = dims.index(max(dims))
    place[longest] = (place[longest] + 1) % dims[longest]
    return drawn.at[tuple(place)].set(top_value)


def steps_of(rng, dims, split, smallest, top_value):
    level = 1.0
    for position, shards_of in split:
        heights = jax.random.uniform(jax.random.fold_in(jax.random.fold_in(rng, 6), position), (shards_of,), jnp.float32, smallest / len(split), top_value / len(split))
        level = level * jnp.repeat(jnp.exp(heights), dims[position] // shards_of).reshape((-1,) + (1,) * (len(dims) - 1 - position))
    return level


def gaussian(own_key, extent, scale, limit, shards=(), held_as=jnp.bfloat16):
    array = jax.random.normal(own_key, extent, jnp.float32) * scale
    if len(shards) > 0:
        array = steps_of(own_key, extent, shards, -0.22, 0.18) * array
    return jnp.clip(array, min=-limit, max=limit).astype(held_as)


def setup_inputs(seed: int = 0) -> dict:
    key_list = jax.random.split(jax.random.key(seed), 16)
    return {
        "features": gaussian(key_list[0], (NY, NX, C), 1.0, 6.0, ((0, 8), (1, 32))),
        "land_mask": set_ends((jax.random.randint(key_list[1], (NY, NX), 0, 4) < 3).astype(jnp.int32), jax.random.fold_in(key_list[1], 1), 0, 1),
        "dw_weight": gaussian(key_list[2], (KS, KS, C), (KS * KS) ** -0.5, 0.875, (), jnp.float32),
        "dw_bias": gaussian(key_list[3], (C,), 0.5, 3.0, (), jnp.float32),
        "norm_gain": jnp.clip(1.0 + 0.15 * jax.random.normal(key_list[4], (C,), jnp.float32), 0.25, 1.75),
        "norm_shift": gaussian(key_list[5], (C,), 0.5, 3.0, (), jnp.float32),
        "expand_weight": gaussian(key_list[6], (C, HID), C ** -0.5, 0.5),
        "expand_bias": gaussian(key_list[7], (HID,), 0.5, 3.0, (), jnp.float32),
        "project_weight": gaussian(key_list[8], (HID, C), HID ** -0.5, 0.25),
        "project_bias": gaussian(key_list[9], (C,), 0.5, 3.0, (), jnp.float32),
        "layer_scale": jnp.clip(jnp.exp(jax.random.uniform(key_list[10], (C,), jnp.float32, math.log(0.3), math.log(1.0))), 0.3, 1.0),
        "out_gain": jnp.clip(1.0 + 0.15 * jax.random.normal(key_list[11], (C,), jnp.float32), 0.25, 1.75),
        "out_shift": gaussian(key_list[12], (C,), 0.5, 3.0, (), jnp.float32),
        "coarse_weight": gaussian(key_list[13], (4, 4, C, OUT), (16 * C) ** -0.5, 0.125),
        "coarse_bias": gaussian(key_list[14], (OUT,), 0.5, 3.0, (), jnp.float32),
    }


def layer_norm(values, gain, shift):
    center = values - lax.optimization_barrier(jnp.mean(values, axis=-1, keepdims=True))
    spread = lax.optimization_barrier(jnp.mean(center * center, axis=-1, keepdims=True))
    return center * lax.rsqrt(spread + 1e-06) * gain + shift

def extend_global(grid_field, rim_size):
    widened = jnp.concatenate([grid_field[:, -rim_size:], grid_field, grid_field[:, :rim_size]], axis=1)
    north_rim = widened[-rim_size:][::-1, ::-1]
    south_rim = jnp.zeros_like(widened[:rim_size])
    return jnp.concatenate([south_rim, widened, north_rim], axis=0)

def convnext_cells(padded_in, centre, land_mask, dw_weight, dw_bias, norm_gain, norm_shift, expand_weight, expand_bias, project_weight, project_bias, layer_scale, out_gain, out_shift):
    height, breadth, channels = centre.shape
    spatial = jnp.zeros(centre.shape, jnp.float32) + dw_bias
    for row_tap in range(dw_weight.shape[0]):
        for col_tap in range(dw_weight.shape[1]):
            spatial = spatial + padded_in[row_tap:row_tap + height, col_tap:col_tap + breadth].astype(jnp.float32) * dw_weight[row_tap, col_tap]
    normed = layer_norm(spatial, norm_gain, norm_shift).astype(jnp.bfloat16).reshape(-1, channels)
    hidden = jax.nn.gelu(jnp.dot(normed, expand_weight, preferred_element_type=jnp.float32) + expand_bias, approximate=False).astype(jnp.bfloat16)
    updated = centre.reshape(-1, channels).astype(jnp.float32) + layer_scale * (jnp.dot(hidden, project_weight, preferred_element_type=jnp.float32) + project_bias)
    marks = land_mask.reshape(-1, 1).astype(jnp.float32)
    normalized = marks * layer_norm(updated, out_gain, out_shift)
    return normalized.astype(jnp.bfloat16).reshape(height, breadth, channels)

def shrink_cells(padded, coarse_weight, coarse_bias):
    height = padded.shape[0] - 2
    breadth = padded.shape[1] - 2
    channels = padded.shape[2]
    total = jnp.zeros((height // 2 * (breadth // 2), coarse_weight.shape[3]), jnp.float32) + coarse_bias
    for row_tap in range(4):
        for col_tap in range(4):
            window = padded[row_tap:row_tap + height:2, col_tap:col_tap + breadth:2].reshape(-1, channels)
            total = total + jnp.dot(window, coarse_weight[row_tap, col_tap], preferred_element_type=jnp.float32)
    return total.astype(jnp.bfloat16).reshape(height // 2, breadth // 2, coarse_weight.shape[3])

def reference(features, land_mask, dw_weight, dw_bias, norm_gain, norm_shift, expand_weight, expand_bias, project_weight, project_bias, layer_scale, out_gain, out_shift, coarse_weight, coarse_bias):
    padded_in = extend_global(features, 3)

    def block_rows(block_index):
        offset = (block_index * CY).astype(jnp.int32)
        rows_in = lax.dynamic_slice_in_dim(padded_in, offset, CY + 6, 0)
        centre = lax.dynamic_slice_in_dim(features, offset, CY, 0)
        marks = lax.dynamic_slice_in_dim(land_mask, offset, CY, 0)
        return convnext_cells(rows_in, centre, marks, dw_weight, dw_bias, norm_gain, norm_shift, expand_weight, expand_bias, project_weight, project_bias, layer_scale, out_gain, out_shift)
    normalized = lax.map(block_rows, jnp.arange(N_LAT, dtype=jnp.int32)).reshape(NY, NX, C)
    padded_out = extend_global(normalized, 1)

    def coarse_rows(block_index):
        offset = (block_index * CY).astype(jnp.int32)
        rows_in = lax.dynamic_slice_in_dim(padded_out, offset, CY + 2, 0)
        return shrink_cells(rows_in, coarse_weight, coarse_bias)
    coarse = lax.map(coarse_rows, jnp.arange(N_LAT, dtype=jnp.int32))
    return coarse.reshape(NY // 2, NX // 2, OUT)
```

```python
import functools

import jax
import jax.numpy as jnp
from jax import lax
from jax.experimental import pallas as pl
from jax.experimental.pallas import tpu as pltpu
from jax.sharding import PartitionSpec as P

F32 = jnp.float32
BF16 = jnp.bfloat16
RIM = 4
LEFT = 8


def dot(a, b):
    return jnp.dot(a, b, preferred_element_type=F32)


def block_kernel(
    feat,
    west,
    east,
    south,
    north,
    marks,
    taps,
    fold_taps,
    dw_bias,
    dw_centred,
    norm_gain,
    norm_shift,
    expand,
    expand_bias,
    project,
    project_bias,
    out_gain,
    out_shift,
    coarse_w,
    coarse_b,
    out,
    field,
    shifted,
    centre_buf,
    norm_buf,
    coarse_in,
):
    rows, cols, chan = feat.shape
    pairs = rows // 2 + 1
    span = shifted.shape[1]
    size = 7

    field[...] = jnp.zeros_like(field)
    field[RIM : RIM + rows, LEFT : LEFT + cols] = feat[...].astype(F32)
    field[RIM : RIM + rows, LEFT - RIM : LEFT] = west[...].astype(F32)
    field[RIM : RIM + rows, LEFT + cols : LEFT + cols + RIM] = east[...].astype(F32)
    field[:RIM, LEFT - RIM : LEFT + cols + RIM] = south[...].astype(F32)
    field[RIM + rows :, LEFT - RIM : LEFT + cols + RIM] = north[...].astype(F32)

    @pl.loop(0, pairs + 3)
    def _(p):
        for b in range(size):
            for g in range(2):
                lane = b * 2 * chan + g * chan
                shifted[p, :, lane : lane + chan] = field[
                    2 * p + g, b + LEFT - RIM : b + LEFT - RIM + span
                ].astype(BF16)

    both = (2 * chan, 2 * chan)
    row_id = lax.broadcasted_iota(jnp.int32, both, 0)
    col_id = lax.broadcasted_iota(jnp.int32, both, 1)
    average = jnp.where(
        (row_id < chan) == (col_id < chan), F32(1.0 / chan), F32(0.0)
    ).astype(BF16)
    mark_row = lax.broadcasted_iota(jnp.int32, (chan, 2 * chan), 0)
    mark_half = (lax.broadcasted_iota(jnp.int32, (chan, 2 * chan), 1) >= chan).astype(jnp.int32)
    mid = 3 * 2 * chan

    @pl.loop(0, pairs)
    def _(q):
        total = dot(shifted[q], taps[0])
        for k in range(1, 4):
            total = total + dot(shifted[q + k], taps[k])
        centre_buf[...] = total + dw_centred[...]

        @pl.when(q == pairs - 1)
        def _():
            acc = jnp.zeros((span, chan), F32) + dw_bias[...]
            for a in range(size):
                for b in range(size):
                    acc = acc + field[
                        rows + 1 + a, b + LEFT - RIM : b + LEFT - RIM + span
                    ] * fold_taps[a, b : b + 1]
            acc = acc - jnp.mean(acc, axis=-1, keepdims=True)
            centre_buf[:, chan:] = acc

        centred = centre_buf[...]
        spread = dot((centred * centred).astype(BF16), average)
        normed = (centred * lax.rsqrt(spread + 1e-06) * norm_gain[...] + norm_shift[...]).astype(
            BF16
        )
        for h in range(2):
            pre = dot(normed[:, h * chan : (h + 1) * chan], expand[...]) + expand_bias[...]
            hidden = (0.5 * pre * (1.0 + lax.erf(pre * (0.5**0.5)))).astype(BF16)
            own = shifted[q + 1 + h, :, mid + (1 - h) * chan : mid + (2 - h) * chan]
            centre_buf[:, h * chan : (h + 1) * chan] = dot(
                jnp.concatenate([hidden, own], axis=1), project[...]
            )
        updated = centre_buf[...] + project_bias[...]
        spread = dot((updated * updated).astype(BF16), average)
        chosen = (mark_row == 2 * q + mark_half).astype(F32).astype(BF16)
        mark = dot(marks[...], chosen)
        normalized = mark * (
            updated * lax.rsqrt(spread + 1e-06) * out_gain[...] + out_shift[...]
        )
        for h in range(2):
            norm_buf[h] = normalized[:, h * chan : (h + 1) * chan]
            for b in range(4):
                lane = b * 2 * chan + h * chan
                coarse_in[q, :, lane : lane + chan] = norm_buf[
                    h, pl.ds(b, cols // 2, stride=2), :
                ].astype(BF16)

    step = 4
    for i in range(0, pairs - 1, step):
        total = jnp.zeros((step * cols // 2, out.shape[2]), F32) + coarse_b[...]
        for k in range(2):
            for b in range(4):
                kernel = jnp.concatenate([coarse_w[2 * k, b], coarse_w[2 * k + 1, b]], axis=0)
                window = coarse_in[i + k : i + k + step, :, b * 2 * chan : (b + 1) * 2 * chan]
                total = total + dot(window.reshape(-1, 2 * chan), kernel)
        out[i : i + step] = total.astype(BF16).reshape(step, cols // 2, out.shape[2])


def halo(features, land_mask):
    rows, cols, chan = features.shape
    marks = land_mask.astype(BF16)
    n_lat = lax.axis_size("lat")
    n_lon = lax.axis_size("lon")
    around = [(i, (i + 1) % n_lon) for i in range(n_lon)]
    back = [(j, i) for i, j in around]

    def with_column(band, column):
        extra = jnp.pad(column[None, None, :], ((0, 0), (0, RIM - 1), (0, chan - rows)))
        return jnp.concatenate([band, extra], axis=0)

    west = lax.ppermute(with_column(features[:, cols - RIM :], marks[:, cols - 1]), "lon", around)
    east = lax.ppermute(with_column(features[:, :RIM], marks[:, 0]), "lon", back)
    wide = jnp.concatenate([west[rows, 0, :rows, None], marks, east[rows, 0, :rows, None]], axis=1)
    west, east = west[:rows], east[:rows]

    def band(start, row, turned):
        cut = slice(start, start + RIM)
        cells = jnp.concatenate([west[cut], features[cut], east[cut]], axis=1)
        line = wide[row]
        if turned:
            cells, line = cells[::-1, ::-1], line[::-1]
        extra = jnp.pad(line, (0, 2 * chan - cols - 2)).reshape(1, 2, chan)
        extra = jnp.pad(extra, ((0, RIM - 1), (0, 0), (0, 0)))
        return jnp.concatenate([cells, extra], axis=1)

    up = [(i, i + 1) for i in range(n_lat - 1)]
    top = (n_lat - 1) * n_lon
    mirror = [(top + i, top + n_lon - 1 - i) for i in range(n_lon)]
    south = lax.ppermute(band(rows - RIM, rows - 1, False), "lat", up)
    north = lax.ppermute(band(0, 0, False), "lat", [(j, i) for i, j in up])
    fold = lax.ppermute(band(rows - RIM, rows - 1, True), ("lat", "lon"), mirror)
    north = north + fold
    width = cols + 2 * RIM

    def line_of(packed):
        return packed[0, width:].reshape(1, -1)[:, : cols + 2]

    all_marks = jnp.concatenate([line_of(south), wide, line_of(north)], axis=0)
    return west, east, south[:, :width], north[:, :width], all_marks


def local(
    features,
    land_mask,
    dw_weight,
    dw_bias,
    norm_gain,
    norm_shift,
    expand_weight,
    expand_bias,
    project_weight,
    project_bias,
    layer_scale,
    out_gain,
    out_shift,
    coarse_weight,
    coarse_bias,
):
    rows, cols, chan = features.shape
    size = dw_weight.shape[0]
    span = -(-(cols + 2) // 16) * 16
    pairs = rows // 2 + 1
    west, east, south, north, all_marks = halo(features, land_mask)
    marks = jnp.pad(all_marks.T, ((0, span - cols - 2), (0, chan - rows - 2)))

    padded = jnp.pad(dw_weight, ((1, 1), (0, 0), (0, 0)))

    def column(h):
        picked = [jnp.stack([padded[2 * k + g - h + 1] for g in range(2)], axis=1) for k in range(4)]
        return jnp.stack(picked).reshape(4, size * 2 * chan, 1)

    lane = lax.broadcasted_iota(jnp.int32, (1, size * 2 * chan, 2 * chan), 2)
    deep = lax.broadcasted_iota(jnp.int32, (1, size * 2 * chan, 2 * chan), 1)
    centring = jnp.where(lane % chan == deep % chan, F32(1.0), F32(0.0)) - F32(1.0 / chan)
    taps = (jnp.where(lane < chan, column(0), column(1)) * centring).astype(BF16)

    at_top = lax.axis_index("lat") == lax.axis_size("lat") - 1
    fold_taps = jnp.where(at_top, dw_weight[::-1, ::-1], dw_weight)

    def twice(vector):
        return jnp.concatenate([vector, vector])[None]

    small = jnp.eye(chan, dtype=F32) - F32(1.0 / chan)
    scaled = project_weight.astype(F32) * layer_scale
    scaled = scaled - jnp.mean(scaled, axis=1, keepdims=True)
    project = jnp.concatenate([scaled, small], axis=0).astype(BF16)
    shift = project_bias * layer_scale
    shift = shift - jnp.mean(shift)

    operands = (
        features,
        west,
        east,
        south,
        north,
        marks,
        taps,
        fold_taps,
        dw_bias[None],
        twice(dw_bias - jnp.mean(dw_bias)),
        twice(norm_gain),
        twice(norm_shift),
        expand_weight,
        expand_bias[None],
        project,
        twice(shift),
        twice(out_gain),
        twice(out_shift),
        coarse_weight,
        coarse_bias[None],
    )
    out_count = coarse_weight.shape[3]
    vmem = pl.BlockSpec(memory_space=pltpu.VMEM)
    return pl.pallas_call(
        block_kernel,
        out_shape=jax.ShapeDtypeStruct((rows // 2, cols // 2, out_count), BF16),
        in_specs=[vmem] * len(operands),
        out_specs=vmem,
        scratch_shapes=[
            pltpu.VMEM((rows + 2 * RIM, span + 16, chan), F32),
            pltpu.VMEM((pairs + 3, span, size * 2 * chan), BF16),
            pltpu.VMEM((span, 2 * chan), F32),
            pltpu.VMEM((2, span, chan), F32),
            pltpu.VMEM((pairs, cols // 2, 8 * chan), BF16),
        ],
        compiler_params=pltpu.CompilerParams(vmem_limit_bytes=60000 * 1024),
        name="block",
    )(*operands)


def solution(mesh):
    placed = (
        P("lat", "lon", None),
        P("lat", "lon"),
    ) + (P(),) * 13
    return jax.shard_map(
        local, mesh=mesh, in_specs=placed, out_specs=P("lat", "lon", None), check_vma=False
    )
```

```python
import jax
import jax.numpy as jnp
from jax import lax
from jax.experimental import pallas as pl
from jax.experimental.pallas import tpu as pltpu
from jax.sharding import PartitionSpec as P

F32 = jnp.float32
BF16 = jnp.bfloat16
RIM = 4
LEFT = 8
SIZE = 7
SPAN = 144
GROUP = 4


def dot(a, b):
    return jnp.dot(a, b, preferred_element_type=F32)


def spread_rows(field, shifted, count, chan):
    @pl.loop(0, count)
    def _(p):
        for b in range(SIZE):
            for g in range(2):
                lane = (2 * b + g) * chan
                start = b + LEFT - RIM
                shifted[p, :, lane : lane + chan] = field[2 * p + g, start : start + SPAN].astype(
                    BF16
                )


def build_taps(dw, taps):
    chan = dw.shape[1]
    square = (chan, chan)
    same = lax.broadcasted_iota(jnp.int32, square, 0) == lax.broadcasted_iota(jnp.int32, square, 1)
    centring = jnp.where(same, F32(1.0), F32(0.0)) - F32(1.0 / chan)
    table = jnp.concatenate(
        [dw[...], jnp.zeros((chan - SIZE * SIZE, chan), F32)], axis=0
    ).T
    nothing = jnp.zeros(square, BF16)
    for b in range(SIZE):
        for a in range(-1, SIZE + 1):
            if 0 <= a < SIZE:
                t = a * SIZE + b
                block = (centring * table[:, t : t + 1]).astype(BF16)
            else:
                block = nothing
            for h in range(2):
                k, g = divmod(a + h, 2)
                if 0 <= a + h <= SIZE:
                    row = ((k * SIZE + b) * 2 + g) * chan
                    taps[row : row + chan, h * chan : (h + 1) * chan] = block


def conv(shifted, starts, taps):
    chan2 = taps.shape[1]
    rhs = taps[...]
    totals = []
    for start in starts:
        lhs = [
            shifted[pl.ds(start + k, 2)].reshape(2 * SPAN, SIZE * chan2) for k in range(4)
        ]
        totals.append(dot(jnp.concatenate(lhs, axis=1), rhs))
    return totals


def average_of(chan):
    both = (2 * chan, 2 * chan)
    row_id = lax.broadcasted_iota(jnp.int32, both, 0)
    col_id = lax.broadcasted_iota(jnp.int32, both, 1)
    return jnp.where(
        (row_id < chan) == (col_id < chan), F32(1.0 / chan), F32(0.0)
    ).astype(BF16)


def two(vector):
    return jnp.concatenate([vector, vector], axis=1)


def centred_row(vector):
    return vector - jnp.mean(vector, axis=-1, keepdims=True)


def cells(centred, own, rows_of, refs, norm_buf, coarse_in, slot, average):
    chan = average.shape[0] // 2
    marks, norm_gain, norm_shift, expand, expand_bias, project, project_bias, out_gain, out_shift = refs
    spread = dot((centred * centred).astype(BF16), average)
    normed = (
        centred * lax.rsqrt(spread + 1e-06) * two(norm_gain[...]) + two(norm_shift[...])
    ).astype(BF16)
    parts = []
    for h in range(2):
        pre = dot(normed[:, h * chan : (h + 1) * chan], expand[...]) + expand_bias[...]
        hidden = (0.5 * pre * (1.0 + lax.erf(pre * (0.5**0.5)))).astype(BF16)
        parts.append(dot(jnp.concatenate([hidden, own[h]], axis=1), project[...]))
    updated = jnp.concatenate(parts, axis=1) + two(project_bias[...])
    spread = dot((updated * updated).astype(BF16), average)
    mark_row = lax.broadcasted_iota(jnp.int32, (chan, chan), 0)
    chosen = jnp.concatenate(
        [(mark_row == r).astype(F32).astype(BF16) for r in rows_of], axis=1
    )
    mark = dot(marks[...].astype(BF16), chosen)
    normalized = mark * (
        updated * lax.rsqrt(spread + 1e-06) * two(out_gain[...]) + two(out_shift[...])
    )
    half = coarse_in.shape[1]
    for h in range(2):
        norm_buf[h] = normalized[:, h * chan : (h + 1) * chan]
    for h in range(2):
        for b in range(4):
            lane = (2 * b + h) * chan
            coarse_in[slot, :, lane : lane + chan] = norm_buf[
                h, pl.ds(b, half, stride=2), :
            ].astype(BF16)


def coarse_rows(coarse_in, first, count, coarse_w, coarse_b):
    total = coarse_b[...]
    for k in range(2):
        kernel = jnp.concatenate(
            [coarse_w[2 * k + h, b] for b in range(4) for h in range(2)], axis=0
        )
        window = coarse_in[first + k : first + k + count]
        total = total + dot(window.reshape(-1, window.shape[2]), kernel)
    return total.astype(BF16).reshape(count, coarse_in.shape[1], -1)


def inner_kernel(
    feat,
    west,
    east,
    land_mask,
    dw,
    dw_bias,
    norm_gain,
    norm_shift,
    expand,
    expand_bias,
    project_w,
    project_b,
    layer_scale,
    out_gain,
    out_shift,
    coarse_w,
    coarse_b,
    out,
    edges,
    taps,
    project,
    project_bias,
    field,
    shifted,
    conv_buf,
    norm_buf,
    coarse_in,
    marks,
):
    rows, cols, chan = feat.shape
    field[:, : LEFT - RIM] = jnp.zeros((rows, LEFT - RIM, chan), F32)
    field[:, LEFT + cols + RIM :] = jnp.zeros((rows, SPAN + 16 - LEFT - cols - RIM, chan), F32)
    field[:, LEFT : LEFT + cols] = feat[...].astype(F32)
    field[:, LEFT - RIM : LEFT] = west[:rows].astype(F32)
    field[:, LEFT + cols : LEFT + cols + RIM] = east[:rows].astype(F32)
    count = shifted.shape[0]
    spread_rows(field, shifted, count, chan)
    build_taps(dw, taps)

    square = (chan, chan)
    same = lax.broadcasted_iota(jnp.int32, square, 0) == lax.broadcasted_iota(jnp.int32, square, 1)
    hid = project_w.shape[0]
    scaled = project_w[...].astype(F32) * layer_scale[...]
    project[:hid] = centred_row(scaled).astype(BF16)
    project[hid:] = (jnp.where(same, F32(1.0), F32(0.0)) - F32(1.0 / chan)).astype(BF16)
    project_bias[...] = centred_row(project_b[...] * layer_scale[...])

    side_table(land_mask, west, east, None, None, marks)
    average = average_of(chan)
    bias = two(centred_row(dw_bias[...]))
    refs = (
        marks,
        norm_gain,
        norm_shift,
        expand,
        expand_bias,
        project,
        project_bias,
        out_gain,
        out_shift,
    )
    mid = (SIZE // 2) * 2 * chan

    @pl.loop(0, (count - 3) // GROUP)
    def _(group):
        base = group * GROUP
        for i, total in enumerate(conv(shifted, [base, base + 2], taps)):
            conv_buf[2 * i : 2 * i + 2] = total.reshape(2, SPAN, 2 * chan) + bias

        @pl.loop(0, GROUP // 2)
        def _(step):
            for j in range(2):
                slot = base + step * 2 + j
                own = [
                    shifted[slot + 1 + h, :, mid + (1 - h) * chan : mid + (2 - h) * chan]
                    for h in range(2)
                ]
                top = 2 * (slot + 2)
                cells(
                    conv_buf[step * 2 + j],
                    own,
                    (top - 1, top),
                    refs,
                    norm_buf.at[j],
                    coarse_in,
                    slot,
                    average,
                )

    done = coarse_in.shape[0] - 1
    for first in range(0, done, 4):
        size = min(4, done - first)
        out[2 + first : 2 + first + size] = coarse_rows(coarse_in, first, size, coarse_w, coarse_b)
    edges[0] = coarse_in[0]
    edges[1] = coarse_in[done]


def side_table(land_mask, west, east, north_line, south_line, marks):
    rows, cols = land_mask.shape

    def neighbour(packed):
        lines = [packed[rows + m] for m in range(rows // RIM)]
        return jnp.concatenate([line.astype(F32) for line in lines], axis=0)

    def turned(block):
        return jnp.concatenate([block, jnp.zeros((cols - rows, cols), F32)], axis=0).T

    own = turned(land_mask[...].astype(F32))
    left = turned(neighbour(west))
    right = turned(neighbour(east))
    marks[cols:, :] = jnp.zeros((SPAN - cols, cols), F32)
    marks[1 : cols + 1, :] = own
    marks[0:1, :] = left[cols - 1 : cols]
    marks[cols + 1 : cols + 2, :] = right[0:1]
    if north_line is not None:
        lines = jnp.concatenate([north_line, south_line, jnp.zeros((cols - 2, 2 * cols), F32)], axis=0)
        tall = jnp.concatenate([lines[:, :cols].T, lines[:, cols:].T], axis=0)[:SPAN]
        lane = lax.broadcasted_iota(jnp.int32, (SPAN, cols), 1)
        moved = jnp.concatenate([tall[:, cols - rows :], tall[:, : cols - rows]], axis=1)
        marks[...] = jnp.where(lane < rows, marks[...], moved)


def outer_kernel(
    feat_low,
    feat_high,
    west,
    east,
    south,
    north,
    fold,
    land_mask,
    dw,
    fold_dw,
    dw_bias,
    norm_gain,
    norm_shift,
    expand,
    expand_bias,
    project_bias,
    out_gain,
    out_shift,
    coarse_b,
    edges,
    project,
    taps_hbm,
    coarse_w_hbm,
    whole_in,
    whole,
    field,
    shifted,
    conv_buf,
    norm_buf,
    coarse_in,
    marks,
    taps,
    coarse_w,
    out_buf,
    shift_buf,
    sems,
):
    del whole_in
    load_taps = pltpu.make_async_copy(taps_hbm, taps, sems.at[0])
    load_coarse = pltpu.make_async_copy(coarse_w_hbm, coarse_w, sems.at[1])
    load_taps.start()
    load_coarse.start()
    low, cols, chan = feat_low.shape
    rows = land_mask.shape[0]
    low = 6
    width = cols + 2 * RIM
    total_rows = field.shape[0]
    field[:, : LEFT - RIM] = jnp.zeros((total_rows, LEFT - RIM, chan), F32)
    field[:, LEFT + cols + RIM :] = jnp.zeros((total_rows, SPAN + 16 - LEFT - cols - RIM, chan), F32)
    field[:RIM, LEFT - RIM : LEFT + cols + RIM] = south[:, :width].astype(F32)
    upper = north[...].astype(F32) + fold[...].astype(F32)
    field[total_rows - RIM :, LEFT - RIM : LEFT + cols + RIM] = upper[:, :width]
    high = RIM + low
    field[RIM:high, LEFT : LEFT + cols] = feat_low[:low].astype(F32)
    field[RIM:high, LEFT - RIM : LEFT] = west[:low].astype(F32)
    field[RIM:high, LEFT + cols : LEFT + cols + RIM] = east[:low].astype(F32)
    field[high : high + 8, LEFT : LEFT + cols] = feat_high[...].astype(F32)
    field[high : high + 8, LEFT - RIM : LEFT] = west[rows - 8 : rows].astype(F32)
    field[high : high + 8, LEFT + cols : LEFT + cols + RIM] = east[rows - 8 : rows].astype(F32)

    def line_of(packed):
        return two_lines(packed[0, width : width + 2])

    def two_lines(pair):
        return jnp.concatenate([pair[0:1], pair[1:2]], axis=1)

    side_table(land_mask, west, east, line_of(upper), line_of(south[...].astype(F32)), marks)
    spread_rows(field, shifted, shifted.shape[0], chan)
    average = average_of(chan)
    bias = two(centred_row(dw_bias[...]))
    shift_buf[...] = project_bias[...]
    refs = (
        marks,
        norm_gain,
        norm_shift,
        expand,
        expand_bias,
        project,
        shift_buf,
        out_gain,
        out_shift,
    )
    mid = (SIZE // 2) * 2 * chan
    load_taps.wait()
    for i, total in enumerate(conv(shifted, [0, 5], taps)):
        conv_buf[2 * i : 2 * i + 2] = total.reshape(2, SPAN, 2 * chan) + bias

    part = SPAN // 2
    first_row = high + 4
    for n in range(0, SPAN, part):
        accs = [jnp.zeros((part, chan), F32) + dw_bias[...] for _ in range(2)]
        for r in range(SIZE + 1):
            for b in range(SIZE):
                start = n + b + LEFT - RIM
                piece = field[first_row + r, start : start + part]
                if r < SIZE:
                    t = r * SIZE + b
                    accs[0] = accs[0] + piece * dw[t : t + 1]
                if r > 0:
                    t = (r - 1) * SIZE + b
                    accs[1] = accs[1] + piece * fold_dw[t : t + 1]
        for h in range(2):
            conv_buf[4, n : n + part, h * chan : (h + 1) * chan] = centred_row(accs[h])

    plan = [
        (0, 0, 0, (rows + 1, 0)),
        (1, 1, 1, (1, 2)),
        (2, 5, 4, (rows - 5, rows - 4)),
        (3, 6, 5, (rows - 3, rows - 2)),
        (4, None, 6, (rows - 1, rows)),
    ]
    for index, at, slot, rows_of in plan:
        if at is None:
            start = SIZE // 2 + LEFT - RIM
            own = [
                field[first_row + 3 + h, start : start + SPAN].astype(BF16) for h in range(2)
            ]
        else:
            own = [
                shifted[at + 1 + h, :, mid + (1 - h) * chan : mid + (2 - h) * chan]
                for h in range(2)
            ]
        cells(
            conv_buf[index], own, rows_of, refs, norm_buf.at[index], coarse_in, slot, average
        )
    coarse_in[2] = edges[0]
    coarse_in[3] = edges[1]
    load_coarse.wait()
    out_buf[:2] = coarse_rows(coarse_in, 0, 2, coarse_w, coarse_b)
    out_buf[2:5] = coarse_rows(coarse_in, 3, 3, coarse_w, coarse_b)
    count = whole.shape[0]
    low_copy = pltpu.make_async_copy(out_buf.at[:2], whole.at[:2], sems.at[0])
    high_copy = pltpu.make_async_copy(out_buf.at[2:5], whole.at[count - 3 : count], sems.at[1])
    low_copy.start()
    high_copy.start()
    low_copy.wait()
    high_copy.wait()


def local(
    features,
    land_mask,
    dw_weight,
    dw_bias,
    norm_gain,
    norm_shift,
    expand_weight,
    expand_bias,
    project_weight,
    project_bias,
    layer_scale,
    out_gain,
    out_shift,
    coarse_weight,
    coarse_bias,
):
    rows, cols, chan = features.shape
    n_lat = lax.axis_size("lat")
    n_lon = lax.axis_size("lon")
    marks = land_mask.astype(BF16)
    extra = marks.reshape(rows // RIM, RIM, cols)
    around = [(i, (i + 1) % n_lon) for i in range(n_lon)]
    back = [(j, i) for i, j in around]
    west = lax.ppermute(
        jnp.concatenate([features[:, cols - RIM :], extra], axis=0), "lon", around
    )
    east = lax.ppermute(jnp.concatenate([features[:, :RIM], extra], axis=0), "lon", back)

    def band(start, row, turned):
        cut = slice(start, start + RIM)
        block = jnp.concatenate([west[cut], features[cut], east[cut]], axis=1)
        place = divmod(row, RIM)
        line = jnp.concatenate(
            [
                west[rows + place[0], place[1], cols - 1 :],
                marks[row],
                east[rows + place[0], place[1], :1],
            ]
        )
        if turned:
            block, line = block[::-1, ::-1], line[::-1]
        tail = jnp.pad(line, (0, 2 * chan - cols - 2)).reshape(1, 2, chan)
        tail = jnp.pad(tail, ((0, RIM - 1), (0, 0), (0, 0)))
        return jnp.concatenate([block, tail], axis=1)

    up = [(i, i + 1) for i in range(n_lat - 1)]
    top = (n_lat - 1) * n_lon
    mirror = [(top + i, top + n_lon - 1 - i) for i in range(n_lon)]
    south = lax.ppermute(band(rows - RIM, rows - 1, False), "lat", up)
    north = lax.ppermute(band(0, 0, False), "lat", [(j, i) for i, j in up])
    fold = lax.ppermute(band(rows - RIM, rows - 1, True), ("lat", "lon"), mirror)

    at_top = lax.axis_index("lat") == n_lat - 1
    dw = dw_weight.reshape(SIZE * SIZE, chan)
    fold_dw = jnp.where(at_top, dw[::-1], dw)
    hid = expand_weight.shape[1]
    out_count = coarse_weight.shape[3]
    half_cols = cols // 2
    whole_shape = jax.ShapeDtypeStruct((rows // 2, half_cols, out_count), BF16)
    vmem = pl.BlockSpec(memory_space=pltpu.VMEM)
    hbm = pl.BlockSpec(memory_space=pl.ANY)
    inner_pairs = rows // 2 - GROUP
    norm_gain, norm_shift, expand_bias, project_bias, layer_scale = (
        v[None] for v in (norm_gain, norm_shift, expand_bias, project_bias, layer_scale)
    )
    out_gain, out_shift, coarse_bias, dw_bias = (
        v[None] for v in (out_gain, out_shift, coarse_bias, dw_bias)
    )
    operands = (
        features,
        west,
        east,
        land_mask,
        dw,
        dw_bias,
        norm_gain,
        norm_shift,
        expand_weight,
        expand_bias,
        project_weight,
        project_bias,
        layer_scale,
        out_gain,
        out_shift,
        coarse_weight,
        coarse_bias,
    )
    whole, edges, taps, project, shift = pl.pallas_call(
        inner_kernel,
        out_shape=(
            whole_shape,
            jax.ShapeDtypeStruct((2, half_cols, 8 * chan), BF16),
            jax.ShapeDtypeStruct((SIZE * 8 * chan, 2 * chan), BF16),
            jax.ShapeDtypeStruct((hid + chan, chan), BF16),
            jax.ShapeDtypeStruct((1, chan), F32),
        ),
        in_specs=[vmem] * len(operands),
        out_specs=(vmem,) * 5,
        scratch_shapes=[
            pltpu.VMEM((rows, SPAN + 16, chan), F32),
            pltpu.VMEM((inner_pairs + 3, SPAN, SIZE * 2 * chan), BF16),
            pltpu.VMEM((GROUP, SPAN, 2 * chan), F32),
            pltpu.VMEM((2, 2, SPAN, chan), F32),
            pltpu.VMEM((inner_pairs, half_cols, 8 * chan), BF16),
            pltpu.VMEM((SPAN, chan), F32),
        ],
        compiler_params=pltpu.CompilerParams(vmem_limit_bytes=40000 * 1024),
        cost_estimate=pl.CostEstimate(
            flops=16_000_000_000, bytes_accessed=8_000_000, transcendentals=0
        ),
        name="inner",
    )(*operands)

    operands = (
        features,
        features,
        west,
        east,
        south,
        north,
        fold,
        land_mask,
        dw,
        fold_dw,
        dw_bias,
        norm_gain,
        norm_shift,
        expand_weight,
        expand_bias,
        shift,
        out_gain,
        out_shift,
        coarse_bias,
        edges,
        project,
        taps,
        coarse_weight,
        whole,
    )
    last = rows // 8 - 1
    specs = [vmem] * (len(operands) - 3) + [hbm] * 3
    specs[0] = pl.BlockSpec((8, cols, chan), lambda i: (0, 0, 0))
    specs[1] = pl.BlockSpec((8, cols, chan), lambda i: (last, 0, 0))
    return pl.pallas_call(
        outer_kernel,
        out_shape=whole_shape,
        grid=(1,),
        in_specs=specs,
        out_specs=hbm,
        scratch_shapes=[
            pltpu.VMEM((22, SPAN + 16, chan), F32),
            pltpu.VMEM((10, SPAN, SIZE * 2 * chan), BF16),
            pltpu.VMEM((5, SPAN, 2 * chan), F32),
            pltpu.VMEM((5, 2, SPAN, chan), F32),
            pltpu.VMEM((7, half_cols, 8 * chan), BF16),
            pltpu.VMEM((SPAN, chan), F32),
            pltpu.VMEM((SIZE * 8 * chan, 2 * chan), BF16),
            pltpu.VMEM(coarse_weight.shape, BF16),
            pltpu.VMEM((5, half_cols, out_count), BF16),
            pltpu.VMEM((1, chan), F32),
            pltpu.SemaphoreType.DMA((2,)),
        ],
        input_output_aliases={len(operands) - 1: 0},
        compiler_params=pltpu.CompilerParams(vmem_limit_bytes=40000 * 1024),
        name="outer",
    )(*operands)


def solution(mesh):
    placed = (
        P("lat", "lon", None),
        P("lat", "lon"),
    ) + (P(),) * 13
    return jax.shard_map(
        local, mesh=mesh, in_specs=placed, out_specs=P("lat", "lon", None), check_vma=False
    )
```

```python
import jax
import jax.numpy as jnp
from jax import lax
from jax.experimental import pallas as pl
from jax.experimental.pallas import tpu as pltpu
from jax.sharding import PartitionSpec as P

F32 = jnp.float32
BF16 = jnp.bfloat16
RIM = 4
LEFT = 8
SIZE = 7
SPAN = 144
GROUP = 4


def dot(a, b):
    return jnp.dot(a, b, preferred_element_type=F32)


def spread_rows(field, shifted, count, chan):
    @pl.loop(0, count)
    def _(p):
        for b in range(SIZE):
            for g in range(2):
                lane = (2 * b + g) * chan
                start = b + LEFT - RIM
                shifted[p, :, lane : lane + chan] = field[2 * p + g, start : start + SPAN].astype(
                    BF16
                )


def centring(chan):
    square = (chan, chan)
    same = lax.broadcasted_iota(jnp.int32, square, 0) == lax.broadcasted_iota(jnp.int32, square, 1)
    return jnp.where(same, F32(1.0), F32(0.0)) - F32(1.0 / chan)


def build_taps(dw, taps):
    chan = dw.shape[2]
    matrix = centring(chan)
    nothing = jnp.zeros((chan, chan), BF16)
    for b in range(SIZE):
        for a in range(-1, SIZE + 1):
            if 0 <= a < SIZE:
                block = (matrix * dw[a, b : b + 1]).astype(BF16)
            else:
                block = nothing
            for h in range(2):
                k, g = divmod(a + h, 2)
                if 0 <= a + h <= SIZE:
                    place = ((k * SIZE + b) * 2 + g) * chan
                    taps[h * chan : (h + 1) * chan, place : place + chan] = block


def conv(shifted, starts, taps):
    chan2 = taps.shape[0]
    rhs = taps[...]
    totals = []
    for start in starts:
        lhs = [
            shifted[pl.ds(start + k, 2)].reshape(2 * SPAN, SIZE * chan2) for k in range(4)
        ]
        totals.append(
            lax.dot_general(
                jnp.concatenate(lhs, axis=1),
                rhs,
                (((1,), (1,)), ((), ())),
                preferred_element_type=F32,
            )
        )
    return totals


def average_of(chan):
    both = (2 * chan, 2 * chan)
    row_id = lax.broadcasted_iota(jnp.int32, both, 0)
    col_id = lax.broadcasted_iota(jnp.int32, both, 1)
    return jnp.where(
        (row_id < chan) == (col_id < chan), F32(1.0 / chan), F32(0.0)
    ).astype(BF16)


def two(vector):
    return jnp.concatenate([vector, vector], axis=1)


def centred_row(vector):
    return vector - jnp.mean(vector, axis=-1, keepdims=True)


def cells(streams, refs, norm_buf, coarse_in, average):
    chan = average.shape[0] // 2
    marks, norm_gain, norm_shift, expand, expand_bias, project, project_bias, out_gain, out_shift = refs
    half = coarse_in.shape[1]
    mark_row = lax.broadcasted_iota(jnp.int32, (chan, chan), 0)
    table = marks[...].astype(BF16)
    centred = [s[0] for s in streams]
    spread = [dot((c * c).astype(BF16), average) for c in centred]
    gain, shift = two(norm_gain[...]), two(norm_shift[...])
    normed = [
        (c * lax.rsqrt(v + 1e-06) * gain + shift).astype(BF16) for c, v in zip(centred, spread)
    ]
    parts = [[] for _ in streams]
    for h in range(2):
        for i, s in enumerate(streams):
            pre = dot(normed[i][:, h * chan : (h + 1) * chan], expand[...]) + expand_bias[...]
            hidden = (0.5 * pre * (1.0 + lax.erf(pre * (0.5**0.5)))).astype(BF16)
            parts[i].append(dot(jnp.concatenate([hidden, s[1][h]], axis=1), project[...]))
    bias = two(project_bias[...])
    updated = [jnp.concatenate(p, axis=1) + bias for p in parts]
    spread = [dot((u * u).astype(BF16), average) for u in updated]
    gain, shift = two(out_gain[...]), two(out_shift[...])
    for i, s in enumerate(streams):
        mark = []
        for rows_of in s[2]:
            chosen = jnp.concatenate(
                [(mark_row == r).astype(F32).astype(BF16) for r in rows_of], axis=1
            )
            mark.append(dot(table, chosen))
        mark = jnp.concatenate(mark, axis=0)
        normalized = mark * (updated[i] * lax.rsqrt(spread[i] + 1e-06) * gain + shift)
        for j, slot in enumerate(s[3]):
            for h in range(2):
                buf = norm_buf.at[s[4] + j, h]
                buf[...] = normalized[j * SPAN : (j + 1) * SPAN, h * chan : (h + 1) * chan]
                for b in range(4):
                    lane = (2 * b + h) * chan
                    coarse_in[slot, :, lane : lane + chan] = buf[
                        pl.ds(b, half, stride=2), :
                    ].astype(BF16)


def coarse_rows(coarse_in, first, count, coarse_w, coarse_b):
    total = coarse_b[...]
    for k in range(2):
        kernel = jnp.concatenate(
            [coarse_w[2 * k + h, b] for b in range(4) for h in range(2)], axis=0
        )
        window = coarse_in[first + k : first + k + count]
        total = total + dot(window.reshape(-1, window.shape[2]), kernel)
    return total.astype(BF16).reshape(count, coarse_in.shape[1], -1)


def own_cells(shifted, at, mid, chan):
    return [
        shifted[
            pl.ds(at + 1 + h, 2), :, mid + (1 - h) * chan : mid + (2 - h) * chan
        ].reshape(2 * SPAN, chan)
        for h in range(2)
    ]


def inner_kernel(
    feat,
    west,
    east,
    land_mask,
    dw,
    dw_bias,
    norm_gain,
    norm_shift,
    expand,
    expand_bias,
    project_w,
    project_b,
    layer_scale,
    out_gain,
    out_shift,
    coarse_w,
    coarse_b,
    out,
    pool,
    field,
    shifted,
    norm_buf,
    coarse_in,
    marks,
    project,
    project_bias,
):
    rows, cols, chan = feat.shape
    taps = pool.at[:, : SIZE * 8 * chan]
    field[:, : LEFT - RIM] = jnp.zeros((rows, LEFT - RIM, chan), F32)
    field[:, LEFT + cols + RIM :] = jnp.zeros((rows, SPAN + 16 - LEFT - cols - RIM, chan), F32)
    field[:, LEFT : LEFT + cols] = feat[...].astype(F32)
    field[:, LEFT - RIM : LEFT] = west[:rows].astype(F32)
    field[:, LEFT + cols : LEFT + cols + RIM] = east[:rows].astype(F32)
    count = shifted.shape[0]
    spread_rows(field, shifted, count, chan)
    build_taps(dw, taps)

    hid = project_w.shape[0]
    scaled = project_w[...].astype(F32) * layer_scale[...]
    project[:hid] = centred_row(scaled).astype(BF16)
    project[hid:] = centring(chan).astype(BF16)
    project_bias[...] = centred_row(project_b[...] * layer_scale[...])

    side_table(land_mask, west, east, marks)
    average = average_of(chan)
    bias = two(centred_row(dw_bias[...]))
    refs = (
        marks,
        norm_gain,
        norm_shift,
        expand,
        expand_bias,
        project,
        project_bias,
        out_gain,
        out_shift,
    )
    mid = (SIZE // 2) * 2 * chan

    @pl.loop(0, (count - 3) // GROUP)
    def _(group):
        base = group * GROUP
        streams = []
        for i, total in enumerate(conv(shifted, [base, base + 2], taps)):
            slot = base + 2 * i
            top = 2 * (slot + 2)
            streams.append(
                (
                    total + bias,
                    own_cells(shifted, slot, mid, chan),
                    [(top - 1, top), (top + 1, top + 2)],
                    [slot, slot + 1],
                    2 * i,
                )
            )
        cells(streams, refs, norm_buf, coarse_in, average)

    done = coarse_in.shape[0] - 1
    for first in range(0, done, 4):
        size = min(4, done - first)
        out[2 + first : 2 + first + size] = coarse_rows(coarse_in, first, size, coarse_w, coarse_b)
    first = taps.shape[1]
    depth = 2 * chan
    for block in range(-(-project.shape[0] // depth)):
        part = project[block * depth : (block + 1) * depth]
        lane = first + block * chan
        pool[: part.shape[0], lane : lane + chan] = part
    pool[chan:, first + 2 * chan : first + 3 * chan] = jnp.zeros((chan, chan), BF16)
    first = first + 3 * chan
    half = coarse_in.shape[1]
    for e, slot in enumerate((0, done)):
        for side in range(2):
            row = side * 2 * half + e * half
            pool[row : row + half, first:] = coarse_in[
                slot, :, side * 4 * chan : (side + 1) * 4 * chan
            ]


def side_table(land_mask, west, east, marks):
    rows, cols = land_mask.shape

    def neighbour(packed):
        lines = [packed[rows + m] for m in range(rows // RIM)]
        return jnp.concatenate([line.astype(F32) for line in lines], axis=0)

    def turned(block):
        return jnp.concatenate([block, jnp.zeros((cols - rows, cols), F32)], axis=0).T

    own = turned(land_mask[...].astype(F32))
    left = turned(neighbour(west))
    right = turned(neighbour(east))
    marks[cols:, :] = jnp.zeros((SPAN - cols, cols), F32)
    marks[1 : cols + 1, :] = own
    marks[0:1, :] = left[cols - 1 : cols]
    marks[cols + 1 : cols + 2, :] = right[0:1]

def rim_kernel(lat, feat_low, feat_high, west, east, land_mask, swap_a, swap_b, block):
    rows, cols = land_mask.shape
    chan = feat_low.shape[2]
    parity = lat[0] % 2
    deep = lax.broadcasted_iota(jnp.int32, (SPAN, cols), 1)
    place = lax.broadcasted_iota(jnp.int32, (SPAN, cols), 0)
    ones = jnp.ones((cols, chan), BF16)

    def fill(feat, first, row):
        block[:RIM, RIM : RIM + cols] = feat[...].astype(F32)
        block[:RIM, :RIM] = west[first : first + RIM].astype(F32)
        block[:RIM, RIM + cols : 2 * RIM + cols] = east[first : first + RIM].astype(F32)
        block[:RIM, 2 * RIM + cols :] = jnp.zeros((RIM, SPAN - 2 * RIM - cols, chan), F32)
        at, part = divmod(row, RIM)
        left = west[rows + at].astype(F32)[part : part + 1]
        right = east[rows + at].astype(F32)[part : part + 1]
        line = land_mask[row : row + 1].astype(F32)
        zero = jnp.zeros((SPAN, cols), F32)
        table = (
            jnp.where(deep == place - RIM, line, zero)
            + jnp.where((place == RIM - 1) & (deep == cols - 1), left, zero)
            + jnp.where((place == RIM + cols) & (deep == 0), right, zero)
        )
        block[RIM] = dot(table.astype(BF16), ones)

    fill(feat_high, rows - RIM, rows - 1)

    @pl.when(parity == 0)
    def _():
        swap_a[...] = block[...].astype(BF16)

    @pl.when(parity == 1)
    def _():
        swap_b[...] = block[...].astype(BF16)

    @pl.when(lat[0] == lat[1])
    def _():
        width = cols + 2 * RIM
        wide = (SPAN, SPAN)
        total = lax.broadcasted_iota(jnp.int32, wide, 0) + lax.broadcasted_iota(jnp.int32, wide, 1)
        turn = (total == width - 1).astype(F32).astype(BF16)
        for r in range(RIM + 1):
            source = RIM - 1 - r if r < RIM else r
            swap_b[r] = dot(turn, block[source].astype(BF16)).astype(BF16)

    fill(feat_low, 0, 0)

    @pl.when(parity == 0)
    def _():
        swap_b[...] = block[...].astype(BF16)

    @pl.when(parity == 1)
    def _():
        swap_a[...] = block[...].astype(BF16)


def outer_kernel(
    lat,
    feat_low,
    feat_high,
    west,
    east,
    rim_a,
    rim_b,
    land_mask,
    dw,
    dw_bias,
    norm_gain,
    norm_shift,
    expand,
    expand_bias,
    project_b,
    layer_scale,
    out_gain,
    out_shift,
    coarse_b,
    pool_hbm,
    coarse_w_hbm,
    whole_in,
    whole,
    field,
    shifted,
    last_buf,
    norm_buf,
    coarse_in,
    marks,
    pool,
    coarse_w,
    project,
    project_bias,
    out_buf,
    sems,
):
    del whole_in
    load_pool = pltpu.make_async_copy(pool_hbm, pool, sems.at[0])
    load_coarse = pltpu.make_async_copy(coarse_w_hbm, coarse_w, sems.at[1])
    load_pool.start()
    load_coarse.start()
    project_bias[...] = centred_row(project_b[...] * layer_scale[...])
    chan = feat_low.shape[2]
    rows, cols = land_mask.shape
    low = 6
    high = RIM + low
    top = high + 8
    used = top + RIM
    left, right = LEFT - RIM, LEFT + cols + RIM
    field[:, :left] = jnp.zeros((used + 2, left, chan), F32)
    field[:, right:] = jnp.zeros((used + 2, SPAN + 16 - right, chan), F32)

    def place(south, north):
        field[:RIM, left:right] = south[:RIM, : right - left].astype(F32)
        field[top:used, left:right] = north[:RIM, : right - left].astype(F32)
        field[used, left:right] = north[RIM, : right - left].astype(F32)
        field[used + 1, left:right] = south[RIM, : right - left].astype(F32)

    @pl.when(lat[0] % 2 == 0)
    def _():
        place(rim_b, rim_a)

    @pl.when(lat[0] % 2 == 1)
    def _():
        place(rim_a, rim_b)

    @pl.when(lat[0] == 0)
    def _():
        field[:RIM, left:right] = jnp.zeros((RIM, right - left, chan), F32)
        field[used + 1, left:right] = jnp.zeros((right - left, chan), F32)

    field[RIM:high, LEFT : LEFT + cols] = feat_low[:low].astype(F32)
    field[RIM:high, left:LEFT] = west[:low].astype(F32)
    field[RIM:high, LEFT + cols : right] = east[:low].astype(F32)
    field[high:top, LEFT : LEFT + cols] = feat_high[...].astype(F32)
    field[high:top, left:LEFT] = west[rows - 8 : rows].astype(F32)
    field[high:top, LEFT + cols : right] = east[rows - 8 : rows].astype(F32)

    side_table(land_mask, west, east, marks)
    lane = lax.broadcasted_iota(jnp.int32, (SPAN, chan), 1)
    start = LEFT - 1
    table = jnp.where(lane == rows, field[used, start : start + SPAN], marks[...])
    marks[...] = jnp.where(lane == rows + 1, field[used + 1, start : start + SPAN], table)
    spread_rows(field, shifted, shifted.shape[0], chan)

    average = average_of(chan)
    bias = two(centred_row(dw_bias[...]))
    refs = (
        marks,
        norm_gain,
        norm_shift,
        expand,
        expand_bias,
        project,
        project_bias,
        out_gain,
        out_shift,
    )
    mid = (SIZE // 2) * 2 * chan
    part = SPAN // 2
    first_row = high + 4
    turned = lat[0] == lat[1]
    for n in range(0, SPAN, part):
        accs = [jnp.zeros((part, chan), F32) + dw_bias[...] for _ in range(2)]
        for r in range(SIZE + 1):
            for b in range(SIZE):
                start = n + b + left
                piece = field[first_row + r, start : start + part]
                if r < SIZE:
                    accs[0] = accs[0] + piece * dw[r, b : b + 1]
                if r > 0:
                    weight = jnp.where(
                        turned,
                        dw[SIZE - r, SIZE - 1 - b : SIZE - b],
                        dw[r - 1, b : b + 1],
                    )
                    accs[1] = accs[1] + piece * weight
        for h in range(2):
            last_buf[n : n + part, h * chan : (h + 1) * chan] = centred_row(accs[h])

    load_pool.wait()
    taps = pool.at[:, : SIZE * 8 * chan]
    first = taps.shape[1]
    depth = 2 * chan
    for block in range(-(-project.shape[0] // depth)):
        size = min(depth, project.shape[0] - block * depth)
        lane = first + block * chan
        project[block * depth : block * depth + size] = pool[:size, lane : lane + chan]
    first = first + 3 * chan
    half = coarse_in.shape[1]
    for e in range(2):
        for side in range(2):
            row = side * 2 * half + e * half
            coarse_in[2 + e, :, side * 4 * chan : (side + 1) * 4 * chan] = pool[
                row : row + half, first:
            ]
    totals = conv(shifted, [0, 5], taps)
    start = SIZE // 2 + left
    streams = [
        (
            totals[0] + bias,
            own_cells(shifted, 0, mid, chan),
            [(rows + 1, 0), (1, 2)],
            [0, 1],
            0,
        ),
        (
            totals[1] + bias,
            own_cells(shifted, 5, mid, chan),
            [(rows - 5, rows - 4), (rows - 3, rows - 2)],
            [4, 5],
            2,
        ),
        (
            last_buf[...],
            [field[first_row + 3 + h, start : start + SPAN].astype(BF16) for h in range(2)],
            [(rows - 1, rows)],
            [6],
            4,
        ),
    ]
    cells(streams, refs, norm_buf, coarse_in, average)
    load_coarse.wait()
    out_buf[:2] = coarse_rows(coarse_in, 0, 2, coarse_w, coarse_b)
    out_buf[2:5] = coarse_rows(coarse_in, 3, 3, coarse_w, coarse_b)
    count = whole.shape[0]
    low_copy = pltpu.make_async_copy(out_buf.at[:2], whole.at[:2], sems.at[0])
    high_copy = pltpu.make_async_copy(out_buf.at[2:5], whole.at[count - 3 : count], sems.at[1])
    low_copy.start()
    high_copy.start()
    low_copy.wait()
    high_copy.wait()


def local(
    features,
    land_mask,
    dw_weight,
    dw_bias,
    norm_gain,
    norm_shift,
    expand_weight,
    expand_bias,
    project_weight,
    project_bias,
    layer_scale,
    out_gain,
    out_shift,
    coarse_weight,
    coarse_bias,
):
    rows, cols, chan = features.shape
    n_lat = lax.axis_size("lat")
    n_lon = lax.axis_size("lon")
    marks = land_mask.astype(BF16)
    extra = marks.reshape(rows // RIM, RIM, cols)
    around = [(i, (i + 1) % n_lon) for i in range(n_lon)]
    back = [(j, i) for i, j in around]
    west = lax.ppermute(
        jnp.concatenate([features[:, cols - RIM :], extra], axis=0), "lon", around
    )
    east = lax.ppermute(jnp.concatenate([features[:, :RIM], extra], axis=0), "lon", back)

    lat = jnp.stack([lax.axis_index("lat"), jnp.int32(n_lat - 1)])
    last = rows // 8 - 1
    scalars = pl.BlockSpec(memory_space=pltpu.SMEM)
    vmem = pl.BlockSpec(memory_space=pltpu.VMEM)
    hbm = pl.BlockSpec(memory_space=pl.ANY)
    band = jax.ShapeDtypeStruct((RIM + 1, SPAN, chan), BF16)
    swap_a, swap_b = pl.pallas_call(
        rim_kernel,
        out_shape=(band, band),
        grid=(1,),
        in_specs=[
            scalars,
            pl.BlockSpec((RIM, cols, chan), lambda i: (0, 0, 0)),
            pl.BlockSpec((RIM, cols, chan), lambda i: (rows // RIM - 1, 0, 0)),
            vmem,
            vmem,
            vmem,
        ],
        out_specs=(vmem, vmem),
        scratch_shapes=[pltpu.VMEM((RIM + 1, SPAN, chan), F32)],
        compiler_params=pltpu.CompilerParams(vmem_limit_bytes=65000 * 1024),
        name="rims",
    )(lat, features, features, west, east, land_mask)
    pairs_a = [(i ^ 1, i) for i in range(n_lat)]
    pairs_b = []
    for i in range(n_lat):
        for j in range(n_lon):
            if i == 0:
                to = (0, j)
            elif i == n_lat - 1:
                to = (i, n_lon - 1 - j)
            else:
                to = (((i + 1) ^ 1) - 1, j)
            pairs_b.append((i * n_lon + j, to[0] * n_lon + to[1]))
    rim_a = lax.ppermute(swap_a, "lat", pairs_a)
    rim_b = lax.ppermute(swap_b, ("lat", "lon"), pairs_b)

    hid = expand_weight.shape[1]
    out_count = coarse_weight.shape[3]
    half_cols = cols // 2
    pool_shape = jax.ShapeDtypeStruct((2 * chan, SIZE * 8 * chan + 7 * chan), BF16)
    whole_shape = jax.ShapeDtypeStruct((rows // 2, half_cols, out_count), BF16)
    inner_pairs = rows // 2 - GROUP
    norm_gain, norm_shift, expand_bias, project_bias, layer_scale = (
        v[None] for v in (norm_gain, norm_shift, expand_bias, project_bias, layer_scale)
    )
    out_gain, out_shift, coarse_bias, dw_bias = (
        v[None] for v in (out_gain, out_shift, coarse_bias, dw_bias)
    )
    operands = (
        features,
        west,
        east,
        land_mask,
        dw_weight,
        dw_bias,
        norm_gain,
        norm_shift,
        expand_weight,
        expand_bias,
        project_weight,
        project_bias,
        layer_scale,
        out_gain,
        out_shift,
        coarse_weight,
        coarse_bias,
    )
    whole, pool = pl.pallas_call(
        inner_kernel,
        out_shape=(
            whole_shape,
            pool_shape,
        ),
        in_specs=[vmem] * len(operands),
        out_specs=(vmem,) * 2,
        scratch_shapes=[
            pltpu.VMEM((rows, SPAN + 16, chan), F32),
            pltpu.VMEM((inner_pairs + 3, SPAN, SIZE * 2 * chan), BF16),
            pltpu.VMEM((GROUP, 2, SPAN, chan), F32),
            pltpu.VMEM((inner_pairs, half_cols, 8 * chan), BF16),
            pltpu.VMEM((SPAN, chan), F32),
            pltpu.VMEM((hid + chan, chan), BF16),
            pltpu.VMEM((1, chan), F32),
        ],
        compiler_params=pltpu.CompilerParams(vmem_limit_bytes=60000 * 1024),
        cost_estimate=pl.CostEstimate(
            flops=16_000_000_000, bytes_accessed=8_000_000, transcendentals=0
        ),
        name="inner",
    )(*operands)

    operands = (
        lat,
        features,
        features,
        west,
        east,
        rim_a,
        rim_b,
        land_mask,
        dw_weight,
        dw_bias,
        norm_gain,
        norm_shift,
        expand_weight,
        expand_bias,
        project_bias,
        layer_scale,
        out_gain,
        out_shift,
        coarse_bias,
        pool,
        coarse_weight,
        whole,
    )
    specs = [vmem] * (len(operands) - 3) + [hbm] * 3
    specs[0] = scalars
    specs[1] = pl.BlockSpec((8, cols, chan), lambda i: (0, 0, 0))
    specs[2] = pl.BlockSpec((8, cols, chan), lambda i: (last, 0, 0))
    return pl.pallas_call(
        outer_kernel,
        out_shape=whole_shape,
        grid=(1,),
        in_specs=specs,
        out_specs=hbm,
        scratch_shapes=[
            pltpu.VMEM((24, SPAN + 16, chan), F32),
            pltpu.VMEM((10, SPAN, SIZE * 2 * chan), BF16),
            pltpu.VMEM((SPAN, 2 * chan), F32),
            pltpu.VMEM((5, 2, SPAN, chan), F32),
            pltpu.VMEM((7, half_cols, 8 * chan), BF16),
            pltpu.VMEM((SPAN, chan), F32),
            pltpu.VMEM(pool_shape.shape, BF16),
            pltpu.VMEM(coarse_weight.shape, BF16),
            pltpu.VMEM((hid + chan, chan), BF16),
            pltpu.VMEM((1, chan), F32),
            pltpu.VMEM((5, half_cols, out_count), BF16),
            pltpu.SemaphoreType.DMA((2,)),
        ],
        input_output_aliases={len(operands) - 1: 0},
        compiler_params=pltpu.CompilerParams(vmem_limit_bytes=64700 * 1024),
        name="outer",
    )(*operands)


def solution(mesh):
    placed = (
        P("lat", "lon", None),
        P("lat", "lon"),
    ) + (P(),) * 13
    return jax.shard_map(
        local, mesh=mesh, in_specs=placed, out_specs=P("lat", "lon", None), check_vma=False
    )
```

```python
import jax
import jax.numpy as jnp
from jax import lax
from jax.experimental import pallas as pl
from jax.experimental.pallas import tpu as pltpu
from jax.sharding import PartitionSpec as P

F32 = jnp.float32
BF16 = jnp.bfloat16
RIM = 4
LEFT = 8
SIZE = 7
SPAN = 144
GROUP = 4


def dot(a, b):
    return jnp.dot(a, b, preferred_element_type=F32)


def spread_rows(field, shifted, count, chan):
    @pl.loop(0, count)
    def _(p):
        for b in range(SIZE):
            for g in range(2):
                lane = (2 * b + g) * chan
                start = b + LEFT - RIM
                shifted[p, :, lane : lane + chan] = field[2 * p + g, start : start + SPAN].astype(
                    BF16
                )


def centring(chan):
    square = (chan, chan)
    same = lax.broadcasted_iota(jnp.int32, square, 0) == lax.broadcasted_iota(jnp.int32, square, 1)
    return jnp.where(same, F32(1.0), F32(0.0)) - F32(1.0 / chan)


def build_taps(dw, taps):
    chan = dw.shape[2]
    matrix = centring(chan)
    nothing = jnp.zeros((chan, chan), BF16)
    for b in range(SIZE):
        for a in range(-1, SIZE + 1):
            if 0 <= a < SIZE:
                block = (matrix * dw[a, b : b + 1]).astype(BF16)
            else:
                block = nothing
            for h in range(2):
                k, g = divmod(a + h, 2)
                if 0 <= a + h <= SIZE:
                    place = ((k * SIZE + b) * 2 + g) * chan
                    taps[h * chan : (h + 1) * chan, place : place + chan] = block


def conv(shifted, starts, taps):
    chan2 = taps.shape[0]
    rhs = taps[...]
    totals = []
    for start in starts:
        lhs = [
            shifted[pl.ds(start + k, 2)].reshape(2 * SPAN, SIZE * chan2) for k in range(4)
        ]
        totals.append(
            lax.dot_general(
                jnp.concatenate(lhs, axis=1),
                rhs,
                (((1,), (1,)), ((), ())),
                preferred_element_type=F32,
            )
        )
    return totals


def average_of(chan):
    both = (2 * chan, 2 * chan)
    row_id = lax.broadcasted_iota(jnp.int32, both, 0)
    col_id = lax.broadcasted_iota(jnp.int32, both, 1)
    return jnp.where(
        (row_id < chan) == (col_id < chan), F32(1.0 / chan), F32(0.0)
    ).astype(BF16)


def two(vector):
    return jnp.concatenate([vector, vector], axis=1)


def centred_row(vector):
    return vector - jnp.mean(vector, axis=-1, keepdims=True)


def cells(streams, refs, norm_buf, coarse_in, average):
    chan = average.shape[0] // 2
    marks, norm_gain, norm_shift, expand, expand_bias, project, project_bias, out_gain, out_shift = refs
    half = coarse_in.shape[1]
    mark_row = lax.broadcasted_iota(jnp.int32, (chan, chan), 0)
    table = marks[...].astype(BF16)
    centred = [s[0] for s in streams]
    spread = [dot((c * c).astype(BF16), average) for c in centred]
    gain, shift = two(norm_gain[...]), two(norm_shift[...])
    normed = [
        (c * lax.rsqrt(v + 1e-06) * gain + shift).astype(BF16) for c, v in zip(centred, spread)
    ]
    parts = [[] for _ in streams]
    for h in range(2):
        for i, s in enumerate(streams):
            pre = dot(normed[i][:, h * chan : (h + 1) * chan], expand[...]) + expand_bias[...]
            hidden = (pre * (1.0 + lax.erf(pre * (0.5**0.5)))).astype(BF16)
            parts[i].append(dot(jnp.concatenate([hidden, s[1][h]], axis=1), project[...]))
    bias = two(project_bias[...])
    updated = [jnp.concatenate(p, axis=1) + bias for p in parts]
    spread = [dot((u * u).astype(BF16), average) for u in updated]
    gain, shift = two(out_gain[...]), two(out_shift[...])
    for i, s in enumerate(streams):
        mark = []
        for rows_of in s[2]:
            chosen = jnp.concatenate(
                [(mark_row == r).astype(F32).astype(BF16) for r in rows_of], axis=1
            )
            mark.append(dot(table, chosen))
        mark = jnp.concatenate(mark, axis=0)
        normalized = mark * (updated[i] * lax.rsqrt(spread[i] + 1e-06) * gain + shift)
        for j, slot in enumerate(s[3]):
            for h in range(2):
                buf = norm_buf.at[s[4] + j, h]
                buf[...] = normalized[j * SPAN : (j + 1) * SPAN, h * chan : (h + 1) * chan]
                for b in range(4):
                    lane = (2 * b + h) * chan
                    coarse_in[slot, :, lane : lane + chan] = buf[
                        pl.ds(b, half, stride=2), :
                    ].astype(BF16)


def coarse_rows(coarse_in, first, count, coarse_w, coarse_b):
    total = coarse_b[...]
    for k in range(2):
        kernel = jnp.concatenate(
            [coarse_w[2 * k + h, b] for b in range(4) for h in range(2)], axis=0
        )
        window = coarse_in[first + k : first + k + count]
        total = total + dot(window.reshape(-1, window.shape[2]), kernel)
    return total.astype(BF16).reshape(count, coarse_in.shape[1], -1)


def own_cells(shifted, at, mid, chan):
    return [
        shifted[
            pl.ds(at + 1 + h, 2), :, mid + (1 - h) * chan : mid + (2 - h) * chan
        ].reshape(2 * SPAN, chan)
        for h in range(2)
    ]


def prepare_kernel(dw, project_w, layer_scale, taps, project):
    hid, chan = project_w.shape
    build_taps(dw, taps)
    scaled = project_w[...].astype(F32) * layer_scale[...]
    project[:hid] = (0.5 * centred_row(scaled)).astype(BF16)
    project[hid:] = centring(chan).astype(BF16)


def inner_kernel(
    feat,
    west,
    east,
    land_mask,
    dw_bias,
    norm_gain,
    norm_shift,
    expand,
    expand_bias,
    project,
    project_b,
    layer_scale,
    out_gain,
    out_shift,
    coarse_b,
    taps_hbm,
    coarse_w_hbm,
    out,
    edges,
    field,
    shifted,
    norm_buf,
    coarse_in,
    marks,
    project_bias,
    conv_buf,
    taps,
    coarse_w,
    sems,
):
    rows, cols, chan = feat.shape
    load_taps = pltpu.make_async_copy(taps_hbm, taps, sems.at[0])
    load_coarse = pltpu.make_async_copy(coarse_w_hbm, coarse_w, sems.at[1])
    load_taps.start()
    load_coarse.start()
    field[:, : LEFT - RIM] = jnp.zeros((rows, LEFT - RIM, chan), F32)
    field[:, LEFT + cols + RIM :] = jnp.zeros((rows, SPAN + 16 - LEFT - cols - RIM, chan), F32)
    field[:, LEFT : LEFT + cols] = feat[...].astype(F32)
    field[:, LEFT - RIM : LEFT] = west[:rows].astype(F32)
    field[:, LEFT + cols : LEFT + cols + RIM] = east[:rows].astype(F32)
    count = shifted.shape[0]
    spread_rows(field, shifted, count, chan)

    project_bias[...] = centred_row(project_b[...] * layer_scale[...])

    side_table(land_mask, west, east, marks)
    average = average_of(chan)
    bias = two(centred_row(dw_bias[...]))
    refs = (
        marks,
        norm_gain,
        norm_shift,
        expand,
        expand_bias,
        project,
        project_bias,
        out_gain,
        out_shift,
    )
    mid = (SIZE // 2) * 2 * chan

    load_taps.wait()

    @pl.loop(0, (count - 3) // GROUP)
    def _(group):
        base = group * GROUP
        streams = []

        @pl.when(group >= 0)
        def _():
            for i, total in enumerate(conv(shifted, [base, base + 2], taps)):
                conv_buf[i] = total + bias

        for i in range(2):
            slot = base + 2 * i
            top = 2 * (slot + 2)
            streams.append(
                (
                    conv_buf[i],
                    own_cells(shifted, slot, mid, chan),
                    [(top - 1, top), (top + 1, top + 2)],
                    [slot, slot + 1],
                    2 * i,
                )
            )
        cells(streams, refs, norm_buf, coarse_in, average)

    done = coarse_in.shape[0] - 1
    load_coarse.wait()
    for first in range(0, done, 4):
        size = min(4, done - first)
        out[2 + first : 2 + first + size] = coarse_rows(coarse_in, first, size, coarse_w, coarse_b)
    edges[0] = coarse_in[0]
    edges[1] = coarse_in[done]


def side_table(land_mask, west, east, marks):
    rows, cols = land_mask.shape

    def neighbour(packed):
        lines = [packed[rows + m] for m in range(rows // RIM)]
        return jnp.concatenate([line.astype(F32) for line in lines], axis=0)

    def turned(block):
        return jnp.concatenate([block, jnp.zeros((cols - rows, cols), F32)], axis=0).T

    own = turned(land_mask[...].astype(F32))
    left = turned(neighbour(west))
    right = turned(neighbour(east))
    marks[cols:, :] = jnp.zeros((SPAN - cols, cols), F32)
    marks[1 : cols + 1, :] = own
    marks[0:1, :] = left[cols - 1 : cols]
    marks[cols + 1 : cols + 2, :] = right[0:1]

def rim_kernel(lat, feat_low, feat_high, west, east, land_mask, swap_a, swap_b, block):
    rows, cols = land_mask.shape
    chan = feat_low.shape[2]
    parity = lat[0] % 2
    deep = lax.broadcasted_iota(jnp.int32, (SPAN, cols), 1)
    place = lax.broadcasted_iota(jnp.int32, (SPAN, cols), 0)
    ones = jnp.ones((cols, chan), BF16)

    def fill(feat, first, row):
        block[:RIM, RIM : RIM + cols] = feat[...].astype(F32)
        block[:RIM, :RIM] = west[first : first + RIM].astype(F32)
        block[:RIM, RIM + cols : 2 * RIM + cols] = east[first : first + RIM].astype(F32)
        block[:RIM, 2 * RIM + cols :] = jnp.zeros((RIM, SPAN - 2 * RIM - cols, chan), F32)
        at, part = divmod(row, RIM)
        left = west[rows + at].astype(F32)[part : part + 1]
        right = east[rows + at].astype(F32)[part : part + 1]
        line = land_mask[row : row + 1].astype(F32)
        zero = jnp.zeros((SPAN, cols), F32)
        table = (
            jnp.where(deep == place - RIM, line, zero)
            + jnp.where((place == RIM - 1) & (deep == cols - 1), left, zero)
            + jnp.where((place == RIM + cols) & (deep == 0), right, zero)
        )
        block[RIM] = dot(table.astype(BF16), ones)

    fill(feat_high, rows - RIM, rows - 1)

    @pl.when(parity == 0)
    def _():
        swap_a[...] = block[...].astype(BF16)

    @pl.when(parity == 1)
    def _():
        swap_b[...] = block[...].astype(BF16)

    @pl.when(lat[0] == lat[1])
    def _():
        width = cols + 2 * RIM
        wide = (SPAN, SPAN)
        total = lax.broadcasted_iota(jnp.int32, wide, 0) + lax.broadcasted_iota(jnp.int32, wide, 1)
        turn = (total == width - 1).astype(F32).astype(BF16)
        for r in range(RIM + 1):
            source = RIM - 1 - r if r < RIM else r
            swap_b[r] = dot(turn, block[source].astype(BF16)).astype(BF16)

    fill(feat_low, 0, 0)

    @pl.when(parity == 0)
    def _():
        swap_b[...] = block[...].astype(BF16)

    @pl.when(parity == 1)
    def _():
        swap_a[...] = block[...].astype(BF16)


def outer_kernel(
    lat,
    feat_low,
    feat_high,
    west,
    east,
    rim_a,
    rim_b,
    land_mask,
    dw,
    dw_bias,
    norm_gain,
    norm_shift,
    expand,
    expand_bias,
    project_b,
    layer_scale,
    out_gain,
    out_shift,
    coarse_b,
    project,
    taps_hbm,
    edges_hbm,
    coarse_w_hbm,
    whole_in,
    whole,
    field,
    shifted,
    last_buf,
    norm_buf,
    coarse_in,
    marks,
    taps,
    coarse_w,
    edges,
    project_bias,
    out_buf,
    conv_buf,
    sems,
):
    del whole_in
    load_taps = pltpu.make_async_copy(taps_hbm, taps, sems.at[0])
    load_edges = pltpu.make_async_copy(edges_hbm, edges, sems.at[2])
    load_coarse = pltpu.make_async_copy(coarse_w_hbm, coarse_w, sems.at[1])
    load_taps.start()
    load_edges.start()
    load_coarse.start()
    project_bias[...] = centred_row(project_b[...] * layer_scale[...])
    chan = feat_low.shape[2]
    rows, cols = land_mask.shape
    low = 6
    high = RIM + low
    top = high + 8
    used = top + RIM
    left, right = LEFT - RIM, LEFT + cols + RIM
    field[:, :left] = jnp.zeros((used + 2, left, chan), F32)
    field[:, right:] = jnp.zeros((used + 2, SPAN + 16 - right, chan), F32)

    def place(south, north):
        field[:RIM, left:right] = south[:RIM, : right - left].astype(F32)
        field[top:used, left:right] = north[:RIM, : right - left].astype(F32)
        field[used, left:right] = north[RIM, : right - left].astype(F32)
        field[used + 1, left:right] = south[RIM, : right - left].astype(F32)

    @pl.when(lat[0] % 2 == 0)
    def _():
        place(rim_b, rim_a)

    @pl.when(lat[0] % 2 == 1)
    def _():
        place(rim_a, rim_b)

    @pl.when(lat[0] == 0)
    def _():
        field[:RIM, left:right] = jnp.zeros((RIM, right - left, chan), F32)
        field[used + 1, left:right] = jnp.zeros((right - left, chan), F32)

    field[RIM:high, LEFT : LEFT + cols] = feat_low[:low].astype(F32)
    field[RIM:high, left:LEFT] = west[:low].astype(F32)
    field[RIM:high, LEFT + cols : right] = east[:low].astype(F32)
    field[high:top, LEFT : LEFT + cols] = feat_high[...].astype(F32)
    field[high:top, left:LEFT] = west[rows - 8 : rows].astype(F32)
    field[high:top, LEFT + cols : right] = east[rows - 8 : rows].astype(F32)

    side_table(land_mask, west, east, marks)
    lane = lax.broadcasted_iota(jnp.int32, (SPAN, chan), 1)
    start = LEFT - 1
    table = jnp.where(lane == rows, field[used, start : start + SPAN], marks[...])
    marks[...] = jnp.where(lane == rows + 1, field[used + 1, start : start + SPAN], table)
    spread_rows(field, shifted, shifted.shape[0], chan)

    average = average_of(chan)
    bias = two(centred_row(dw_bias[...]))
    refs = (
        marks,
        norm_gain,
        norm_shift,
        expand,
        expand_bias,
        project,
        project_bias,
        out_gain,
        out_shift,
    )
    mid = (SIZE // 2) * 2 * chan
    part = SPAN // 2
    first_row = high + 4
    turned = lat[0] == lat[1]
    for n in range(0, SPAN, part):
        accs = [jnp.zeros((part, chan), F32) + dw_bias[...] for _ in range(2)]
        for r in range(SIZE + 1):
            for b in range(SIZE):
                start = n + b + left
                piece = field[first_row + r, start : start + part]
                if r < SIZE:
                    accs[0] = accs[0] + piece * dw[r, b : b + 1]
                if r > 0:
                    weight = jnp.where(
                        turned,
                        dw[SIZE - r, SIZE - 1 - b : SIZE - b],
                        dw[r - 1, b : b + 1],
                    )
                    accs[1] = accs[1] + piece * weight
        for h in range(2):
            last_buf[n : n + part, h * chan : (h + 1) * chan] = centred_row(accs[h])

    load_taps.wait()
    load_edges.wait()
    coarse_in[2] = edges[0]
    coarse_in[3] = edges[1]

    @pl.when(lat[0] >= 0)
    def _():
        for i, total in enumerate(conv(shifted, [0, 5], taps)):
            conv_buf[i] = total + bias

    start = SIZE // 2 + left
    streams = [
        (
            conv_buf[0],
            own_cells(shifted, 0, mid, chan),
            [(rows + 1, 0), (1, 2)],
            [0, 1],
            0,
        ),
        (
            conv_buf[1],
            own_cells(shifted, 5, mid, chan),
            [(rows - 5, rows - 4), (rows - 3, rows - 2)],
            [4, 5],
            2,
        ),
        (
            last_buf[...],
            [field[first_row + 3 + h, start : start + SPAN].astype(BF16) for h in range(2)],
            [(rows - 1, rows)],
            [6],
            4,
        ),
    ]
    cells(streams, refs, norm_buf, coarse_in, average)
    load_coarse.wait()
    out_buf[:2] = coarse_rows(coarse_in, 0, 2, coarse_w, coarse_b)
    out_buf[2:5] = coarse_rows(coarse_in, 3, 3, coarse_w, coarse_b)
    count = whole.shape[0]
    low_copy = pltpu.make_async_copy(out_buf.at[:2], whole.at[:2], sems.at[0])
    high_copy = pltpu.make_async_copy(out_buf.at[2:5], whole.at[count - 3 : count], sems.at[1])
    low_copy.start()
    high_copy.start()
    low_copy.wait()
    high_copy.wait()


def local(
    features,
    land_mask,
    dw_weight,
    dw_bias,
    norm_gain,
    norm_shift,
    expand_weight,
    expand_bias,
    project_weight,
    project_bias,
    layer_scale,
    out_gain,
    out_shift,
    coarse_weight,
    coarse_bias,
):
    rows, cols, chan = features.shape
    n_lat = lax.axis_size("lat")
    n_lon = lax.axis_size("lon")
    marks = land_mask.astype(BF16)
    extra = marks.reshape(rows // RIM, RIM, cols)
    around = [(i, (i + 1) % n_lon) for i in range(n_lon)]
    back = [(j, i) for i, j in around]
    west = lax.ppermute(
        jnp.concatenate([features[:, cols - RIM :], extra], axis=0), "lon", around
    )
    east = lax.ppermute(jnp.concatenate([features[:, :RIM], extra], axis=0), "lon", back)

    lat = jnp.stack([lax.axis_index("lat"), jnp.int32(n_lat - 1)])
    last = rows // 8 - 1
    scalars = pl.BlockSpec(memory_space=pltpu.SMEM)
    vmem = pl.BlockSpec(memory_space=pltpu.VMEM)
    hbm = pl.BlockSpec(memory_space=pl.ANY)
    band = jax.ShapeDtypeStruct((RIM + 1, SPAN, chan), BF16)
    swap_a, swap_b = pl.pallas_call(
        rim_kernel,
        out_shape=(band, band),
        in_specs=[scalars] + [vmem] * 5,
        out_specs=(vmem, vmem),
        scratch_shapes=[pltpu.VMEM((RIM + 1, SPAN, chan), F32)],
        compiler_params=pltpu.CompilerParams(vmem_limit_bytes=8000 * 1024),
        name="rims",
    )(lat, features[:RIM], features[rows - RIM :], west, east, land_mask)
    pairs_a = [(i ^ 1, i) for i in range(n_lat)]
    pairs_b = []
    for i in range(n_lat):
        for j in range(n_lon):
            if i == 0:
                to = (0, j)
            elif i == n_lat - 1:
                to = (i, n_lon - 1 - j)
            else:
                to = (((i + 1) ^ 1) - 1, j)
            pairs_b.append((i * n_lon + j, to[0] * n_lon + to[1]))
    rim_a = lax.ppermute(swap_a, "lat", pairs_a)
    rim_b = lax.ppermute(swap_b, ("lat", "lon"), pairs_b)

    hid = expand_weight.shape[1]
    out_count = coarse_weight.shape[3]
    half_cols = cols // 2
    whole_shape = jax.ShapeDtypeStruct((rows // 2, half_cols, out_count), BF16)
    inner_pairs = rows // 2 - GROUP
    norm_gain, norm_shift, expand_bias, project_bias, layer_scale = (
        v[None] for v in (norm_gain, norm_shift, expand_bias, project_bias, layer_scale)
    )
    out_gain, out_shift, coarse_bias, dw_bias = (
        v[None] for v in (out_gain, out_shift, coarse_bias, dw_bias)
    )
    taps_shape = jax.ShapeDtypeStruct((2 * chan, SIZE * 8 * chan), BF16)
    taps, project = pl.pallas_call(
        prepare_kernel,
        out_shape=(taps_shape, jax.ShapeDtypeStruct((hid + chan, chan), BF16)),
        in_specs=[vmem] * 3,
        out_specs=(vmem,) * 2,
        compiler_params=pltpu.CompilerParams(vmem_limit_bytes=60000 * 1024),
        cost_estimate=pl.CostEstimate(
            flops=2_000_000_000, bytes_accessed=4_000_000, transcendentals=0
        ),
        name="prepare",
    )(dw_weight, project_weight, layer_scale)
    operands = (
        features,
        west,
        east,
        land_mask,
        dw_bias,
        norm_gain,
        norm_shift,
        expand_weight,
        expand_bias,
        project,
        project_bias,
        layer_scale,
        out_gain,
        out_shift,
        coarse_bias,
        taps,
        coarse_weight,
    )
    whole, edges = pl.pallas_call(
        inner_kernel,
        out_shape=(whole_shape, jax.ShapeDtypeStruct((2, half_cols, 8 * chan), BF16)),
        in_specs=[vmem] * (len(operands) - 2) + [hbm] * 2,
        out_specs=(vmem,) * 2,
        scratch_shapes=[
            pltpu.VMEM((rows, SPAN + 16, chan), F32),
            pltpu.VMEM((inner_pairs + 3, SPAN, SIZE * 2 * chan), BF16),
            pltpu.VMEM((GROUP, 2, SPAN, chan), F32),
            pltpu.VMEM((inner_pairs, half_cols, 8 * chan), BF16),
            pltpu.VMEM((SPAN, chan), F32),
            pltpu.VMEM((1, chan), F32),
            pltpu.VMEM((2, 2 * SPAN, 2 * chan), F32),
            pltpu.VMEM(taps_shape.shape, BF16),
            pltpu.VMEM(coarse_weight.shape, BF16),
            pltpu.SemaphoreType.DMA((2,)),
        ],
        compiler_params=pltpu.CompilerParams(vmem_limit_bytes=60000 * 1024),
        cost_estimate=pl.CostEstimate(
            flops=16_000_000_000, bytes_accessed=8_000_000, transcendentals=0
        ),
        name="inner",
    )(*operands)

    operands = (
        lat,
        features,
        features,
        west,
        east,
        rim_a,
        rim_b,
        land_mask,
        dw_weight,
        dw_bias,
        norm_gain,
        norm_shift,
        expand_weight,
        expand_bias,
        project_bias,
        layer_scale,
        out_gain,
        out_shift,
        coarse_bias,
        project,
        taps,
        edges,
        coarse_weight,
        whole,
    )
    specs = [vmem] * (len(operands) - 4) + [hbm] * 4
    specs[0] = scalars
    specs[1] = pl.BlockSpec((8, cols, chan), lambda i: (0, 0, 0))
    specs[2] = pl.BlockSpec((8, cols, chan), lambda i: (last, 0, 0))
    return pl.pallas_call(
        outer_kernel,
        out_shape=whole_shape,
        grid=(1,),
        in_specs=specs,
        out_specs=hbm,
        scratch_shapes=[
            pltpu.VMEM((24, SPAN + 16, chan), F32),
            pltpu.VMEM((10, SPAN, SIZE * 2 * chan), BF16),
            pltpu.VMEM((SPAN, 2 * chan), F32),
            pltpu.VMEM((5, 2, SPAN, chan), F32),
            pltpu.VMEM((7, half_cols, 8 * chan), BF16),
            pltpu.VMEM((SPAN, chan), F32),
            pltpu.VMEM(taps_shape.shape, BF16),
            pltpu.VMEM(coarse_weight.shape, BF16),
            pltpu.VMEM((2, half_cols, 8 * chan), BF16),
            pltpu.VMEM((1, chan), F32),
            pltpu.VMEM((5, half_cols, out_count), BF16),
            pltpu.VMEM((2, 2 * SPAN, 2 * chan), F32),
            pltpu.SemaphoreType.DMA((3,)),
        ],
        input_output_aliases={len(operands) - 1: 0},
        compiler_params=pltpu.CompilerParams(
            vmem_limit_bytes=64700 * 1024,
        ),
        name="outer",
    )(*operands)


def solution(mesh):
    placed = (
        P("lat", "lon", None),
        P("lat", "lon"),
    ) + (P(),) * 13
    return jax.shard_map(
        local, mesh=mesh, in_specs=placed, out_specs=P("lat", "lon", None), check_vma=False
    )
```

```python
import jax
import jax.numpy as jnp
from jax import lax
from jax.experimental import pallas as pl
from jax.experimental.pallas import tpu as pltpu
from jax.sharding import PartitionSpec as P


F32 = jnp.float32
BF16 = jnp.bfloat16
RIM = 4
LEFT = 8
SIZE = 7
SPAN = 144
GROUP = 4


def dot(a, b):
    return jnp.dot(a, b, preferred_element_type=F32)


def spread_rows(field, shifted, count, chan):
    @pl.loop(0, count)
    def _(p):
        for b in range(SIZE):
            for g in range(2):
                lane = (2 * b + g) * chan
                start = b + LEFT - RIM
                shifted[p, :, lane : lane + chan] = field[2 * p + g, start : start + SPAN].astype(
                    BF16
                )


def centring(chan):
    square = (chan, chan)
    same = lax.broadcasted_iota(jnp.int32, square, 0) == lax.broadcasted_iota(jnp.int32, square, 1)
    return jnp.where(same, F32(1.0), F32(0.0)) - F32(1.0 / chan)


def build_taps(dw, taps, finished):
    chan = dw.shape[2]
    matrix = centring(chan)
    nothing = jnp.zeros((chan, chan), BF16)
    for a in range(-1, SIZE + 1):
        for b in range(SIZE):
            if 0 <= a < SIZE:
                block = (matrix * dw[a, b : b + 1]).astype(BF16)
            else:
                block = nothing
            for h in range(2):
                k, g = divmod(a + h, 2)
                if 0 <= a + h <= SIZE:
                    place = ((k * SIZE + b) * 2 + g) * chan
                    taps[h * chan : (h + 1) * chan, place : place + chan] = block
        if a >= 0 and a % 2 == 1:
            finished(a // 2)


def conv(shifted, starts, taps):
    chan2 = taps.shape[0]
    rhs = taps[...]
    totals = []
    for start in starts:
        lhs = [
            shifted[pl.ds(start + k, 2)].reshape(2 * SPAN, SIZE * chan2) for k in range(4)
        ]
        totals.append(
            lax.dot_general(
                jnp.concatenate(lhs, axis=1),
                rhs,
                (((1,), (1,)), ((), ())),
                preferred_element_type=F32,
            )
        )
    return totals


def average_of(chan):
    both = (2 * chan, 2 * chan)
    row_id = lax.broadcasted_iota(jnp.int32, both, 0)
    col_id = lax.broadcasted_iota(jnp.int32, both, 1)
    return jnp.where(
        (row_id < chan) == (col_id < chan), F32(1.0 / chan), F32(0.0)
    ).astype(BF16)


def two(vector):
    return jnp.concatenate([vector, vector], axis=1)


def centred_row(vector):
    return vector - jnp.mean(vector, axis=-1, keepdims=True)


def cells(streams, refs, norm_buf, coarse_in, average):
    chan = average.shape[0] // 2
    marks, norm_gain, norm_shift, expand, expand_bias, project, project_bias, out_gain, out_shift = refs
    half = coarse_in.shape[1]
    mark_row = lax.broadcasted_iota(jnp.int32, (chan, chan), 0)
    table = marks[...].astype(BF16)
    centred = [s[0] for s in streams]
    spread = [dot((c * c).astype(BF16), average) for c in centred]
    gain, shift = two(norm_gain[...]), two(norm_shift[...])
    normed = [
        (c * lax.rsqrt(v + 1e-06) * gain + shift).astype(BF16) for c, v in zip(centred, spread)
    ]
    parts = [[] for _ in streams]
    for h in range(2):
        for i, s in enumerate(streams):
            pre = dot(normed[i][:, h * chan : (h + 1) * chan], expand[...]) + expand_bias[...]
            hidden = (pre * (1.0 + lax.erf(pre * (0.5**0.5)))).astype(BF16)
            parts[i].append(dot(jnp.concatenate([hidden, s[1][h]], axis=1), project[...]))
    bias = two(project_bias[...])
    updated = [jnp.concatenate(p, axis=1) + bias for p in parts]
    spread = [dot((u * u).astype(BF16), average) for u in updated]
    gain, shift = two(out_gain[...]), two(out_shift[...])
    for i, s in enumerate(streams):
        mark = []
        for rows_of in s[2]:
            chosen = jnp.concatenate(
                [(mark_row == r).astype(F32).astype(BF16) for r in rows_of], axis=1
            )
            mark.append(dot(table, chosen))
        mark = jnp.concatenate(mark, axis=0)
        normalized = mark * (updated[i] * lax.rsqrt(spread[i] + 1e-06) * gain + shift)
        for j, slot in enumerate(s[3]):
            for h in range(2):
                buf = norm_buf.at[s[4] + j, h]
                buf[...] = normalized[j * SPAN : (j + 1) * SPAN, h * chan : (h + 1) * chan]
                for b in range(4):
                    lane = (2 * b + h) * chan
                    coarse_in[slot, :, lane : lane + chan] = buf[
                        pl.ds(b, half, stride=2), :
                    ].astype(BF16)


def coarse_rows(coarse_in, first, count, coarse_w, coarse_b):
    total = coarse_b[...]
    for k in range(2):
        kernel = jnp.concatenate(
            [coarse_w[2 * k + h, b] for b in range(4) for h in range(2)], axis=0
        )
        window = coarse_in[first + k : first + k + count]
        total = total + dot(window.reshape(-1, window.shape[2]), kernel)
    return total.astype(BF16).reshape(count, coarse_in.shape[1], -1)


def own_cells(shifted, at, mid, chan):
    return [
        shifted[
            pl.ds(at + 1 + h, 2), :, mid + (1 - h) * chan : mid + (2 - h) * chan
        ].reshape(2 * SPAN, chan)
        for h in range(2)
    ]


def prepare_kernel(dw, project_w, layer_scale, taps_hbm, project, taps, sems):
    hid, chan = project_w.shape
    depth = taps.shape[1] // 4

    def piece(k):
        cut = slice(k * depth, (k + 1) * depth)
        return pltpu.make_async_copy(taps.at[:, cut], taps_hbm.at[:, cut], sems.at[k])

    build_taps(dw, taps, lambda k: piece(k).start())
    scaled = project_w[...].astype(F32) * layer_scale[...]
    project[:hid] = (0.5 * centred_row(scaled)).astype(BF16)
    project[hid:] = centring(chan).astype(BF16)
    for k in range(4):
        piece(k).wait()


def inner_kernel(
    feat,
    west,
    east,
    land_mask,
    dw_bias,
    norm_gain,
    norm_shift,
    expand,
    expand_bias,
    project,
    project_b,
    layer_scale,
    out_gain,
    out_shift,
    coarse_b,
    taps_hbm,
    coarse_w_hbm,
    out,
    edges,
    field,
    shifted,
    norm_buf,
    coarse_in,
    marks,
    project_bias,
    conv_buf,
    taps,
    coarse_w,
    sems,
):
    rows, cols, chan = feat.shape
    load_taps = pltpu.make_async_copy(taps_hbm, taps, sems.at[0])
    load_coarse = pltpu.make_async_copy(coarse_w_hbm, coarse_w, sems.at[1])
    load_taps.start()
    load_coarse.start()
    field[:, : LEFT - RIM] = jnp.zeros((rows, LEFT - RIM, chan), F32)
    field[:, LEFT + cols + RIM :] = jnp.zeros((rows, SPAN + 16 - LEFT - cols - RIM, chan), F32)
    field[:, LEFT : LEFT + cols] = feat[...].astype(F32)
    field[:, LEFT - RIM : LEFT] = west[:rows].astype(F32)
    field[:, LEFT + cols : LEFT + cols + RIM] = east[:rows].astype(F32)
    count = shifted.shape[0]
    spread_rows(field, shifted, count, chan)

    project_bias[...] = centred_row(project_b[...] * layer_scale[...])

    side_table(land_mask, west, east, marks)
    average = average_of(chan)
    bias = two(centred_row(dw_bias[...]))
    refs = (
        marks,
        norm_gain,
        norm_shift,
        expand,
        expand_bias,
        project,
        project_bias,
        out_gain,
        out_shift,
    )
    mid = (SIZE // 2) * 2 * chan

    load_taps.wait()

    @pl.loop(0, (count - 3) // GROUP)
    def _(group):
        base = group * GROUP
        streams = []

        @pl.when(group >= 0)
        def _():
            for i, total in enumerate(conv(shifted, [base, base + 2], taps)):
                conv_buf[i] = total + bias

        for i in range(2):
            slot = base + 2 * i
            top = 2 * (slot + 2)
            streams.append(
                (
                    conv_buf[i],
                    own_cells(shifted, slot, mid, chan),
                    [(top - 1, top), (top + 1, top + 2)],
                    [slot, slot + 1],
                    2 * i,
                )
            )
        cells(streams, refs, norm_buf, coarse_in, average)

    done = coarse_in.shape[0] - 1
    load_coarse.wait()
    for first in range(0, done, 4):
        size = min(4, done - first)
        out[2 + first : 2 + first + size] = coarse_rows(coarse_in, first, size, coarse_w, coarse_b)
    edges[0] = coarse_in[0]
    edges[1] = coarse_in[done]


def side_table(land_mask, west, east, marks):
    rows, cols = land_mask.shape

    def neighbour(packed):
        lines = [packed[rows + m] for m in range(rows // RIM)]
        return jnp.concatenate([line.astype(F32) for line in lines], axis=0)

    def turned(block):
        return jnp.concatenate([block, jnp.zeros((cols - rows, cols), F32)], axis=0).T

    own = turned(land_mask[...].astype(F32))
    left = turned(neighbour(west))
    right = turned(neighbour(east))
    marks[cols:, :] = jnp.zeros((SPAN - cols, cols), F32)
    marks[1 : cols + 1, :] = own
    marks[0:1, :] = left[cols - 1 : cols]
    marks[cols + 1 : cols + 2, :] = right[0:1]


def rim_kernel(lat, feat_low, feat_high, west, east, land_mask, swap_a, swap_b, block):
    rows, cols = land_mask.shape
    chan = feat_low.shape[2]
    parity = lat[0] % 2
    deep = lax.broadcasted_iota(jnp.int32, (SPAN, cols), 1)
    place = lax.broadcasted_iota(jnp.int32, (SPAN, cols), 0)
    ones = jnp.ones((cols, chan), BF16)

    def fill(feat, first, row):
        block[:RIM, RIM : RIM + cols] = feat[...].astype(F32)
        block[:RIM, :RIM] = west[first : first + RIM].astype(F32)
        block[:RIM, RIM + cols : 2 * RIM + cols] = east[first : first + RIM].astype(F32)
        block[:RIM, 2 * RIM + cols :] = jnp.zeros((RIM, SPAN - 2 * RIM - cols, chan), F32)
        at, part = divmod(row, RIM)
        left = west[rows + at].astype(F32)[part : part + 1]
        right = east[rows + at].astype(F32)[part : part + 1]
        line = land_mask[row : row + 1].astype(F32)
        zero = jnp.zeros((SPAN, cols), F32)
        table = (
            jnp.where(deep == place - RIM, line, zero)
            + jnp.where((place == RIM - 1) & (deep == cols - 1), left, zero)
            + jnp.where((place == RIM + cols) & (deep == 0), right, zero)
        )
        block[RIM] = dot(table.astype(BF16), ones)

    fill(feat_high, rows - RIM, rows - 1)

    @pl.when(parity == 0)
    def _():
        swap_a[...] = block[...].astype(BF16)

    @pl.when(parity == 1)
    def _():
        swap_b[...] = block[...].astype(BF16)

    @pl.when(lat[0] == lat[1])
    def _():
        width = cols + 2 * RIM
        wide = (SPAN, SPAN)
        total = lax.broadcasted_iota(jnp.int32, wide, 0) + lax.broadcasted_iota(jnp.int32, wide, 1)
        turn = (total == width - 1).astype(F32).astype(BF16)
        for r in range(RIM + 1):
            source = RIM - 1 - r if r < RIM else r
            swap_b[r] = dot(turn, block[source].astype(BF16)).astype(BF16)

    fill(feat_low, 0, 0)

    @pl.when(parity == 0)
    def _():
        swap_b[...] = block[...].astype(BF16)

    @pl.when(parity == 1)
    def _():
        swap_a[...] = block[...].astype(BF16)


def outer_kernel(
    lat,
    feat_low,
    feat_high,
    west,
    east,
    rim_a,
    rim_b,
    land_mask,
    dw,
    dw_bias,
    norm_gain,
    norm_shift,
    expand,
    expand_bias,
    project_b,
    layer_scale,
    out_gain,
    out_shift,
    coarse_b,
    project,
    taps_hbm,
    edges_hbm,
    coarse_w_hbm,
    whole_in,
    whole,
    field,
    shifted,
    last_buf,
    norm_buf,
    coarse_in,
    marks,
    taps,
    coarse_w,
    edges,
    project_bias,
    out_buf,
    conv_buf,
    sems,
):
    del whole_in
    load_taps = pltpu.make_async_copy(taps_hbm, taps, sems.at[0])
    load_edges = pltpu.make_async_copy(edges_hbm, edges, sems.at[2])
    load_coarse = pltpu.make_async_copy(coarse_w_hbm, coarse_w, sems.at[1])
    load_taps.start()
    load_edges.start()
    load_coarse.start()
    project_bias[...] = centred_row(project_b[...] * layer_scale[...])
    chan = feat_low.shape[2]
    rows, cols = land_mask.shape
    low = 6
    high = RIM + low
    top = high + 8
    used = top + RIM
    left, right = LEFT - RIM, LEFT + cols + RIM
    field[:, :left] = jnp.zeros((used + 2, left, chan), F32)
    field[:, right:] = jnp.zeros((used + 2, SPAN + 16 - right, chan), F32)

    def place(south, north):
        field[:RIM, left:right] = south[:RIM, : right - left].astype(F32)
        field[top:used, left:right] = north[:RIM, : right - left].astype(F32)
        field[used, left:right] = north[RIM, : right - left].astype(F32)
        field[used + 1, left:right] = south[RIM, : right - left].astype(F32)

    @pl.when(lat[0] % 2 == 0)
    def _():
        place(rim_b, rim_a)

    @pl.when(lat[0] % 2 == 1)
    def _():
        place(rim_a, rim_b)

    @pl.when(lat[0] == 0)
    def _():
        field[:RIM, left:right] = jnp.zeros((RIM, right - left, chan), F32)
        field[used + 1, left:right] = jnp.zeros((right - left, chan), F32)

    field[RIM:high, LEFT : LEFT + cols] = feat_low[:low].astype(F32)
    field[RIM:high, left:LEFT] = west[:low].astype(F32)
    field[RIM:high, LEFT + cols : right] = east[:low].astype(F32)
    field[high:top, LEFT : LEFT + cols] = feat_high[...].astype(F32)
    field[high:top, left:LEFT] = west[rows - 8 : rows].astype(F32)
    field[high:top, LEFT + cols : right] = east[rows - 8 : rows].astype(F32)

    side_table(land_mask, west, east, marks)
    lane = lax.broadcasted_iota(jnp.int32, (SPAN, chan), 1)
    start = LEFT - 1
    table = jnp.where(lane == rows, field[used, start : start + SPAN], marks[...])
    marks[...] = jnp.where(lane == rows + 1, field[used + 1, start : start + SPAN], table)
    spread_rows(field, shifted, shifted.shape[0], chan)

    average = average_of(chan)
    bias = two(centred_row(dw_bias[...]))
    refs = (
        marks,
        norm_gain,
        norm_shift,
        expand,
        expand_bias,
        project,
        project_bias,
        out_gain,
        out_shift,
    )
    mid = (SIZE // 2) * 2 * chan
    part = SPAN // 2
    first_row = high + 4
    turned = lat[0] == lat[1]
    for n in range(0, SPAN, part):
        accs = [jnp.zeros((part, chan), F32) + dw_bias[...] for _ in range(2)]
        for r in range(SIZE + 1):
            for b in range(SIZE):
                start = n + b + left
                piece = field[first_row + r, start : start + part]
                if r < SIZE:
                    accs[0] = accs[0] + piece * dw[r, b : b + 1]
                if r > 0:
                    weight = jnp.where(
                        turned,
                        dw[SIZE - r, SIZE - 1 - b : SIZE - b],
                        dw[r - 1, b : b + 1],
                    )
                    accs[1] = accs[1] + piece * weight
        for h in range(2):
            last_buf[n : n + part, h * chan : (h + 1) * chan] = centred_row(accs[h])

    load_taps.wait()
    load_edges.wait()
    coarse_in[2] = edges[0]
    coarse_in[3] = edges[1]

    @pl.when(lat[0] >= 0)
    def _():
        for i, total in enumerate(conv(shifted, [0, 5], taps)):
            conv_buf[i] = total + bias

    start = SIZE // 2 + left
    streams = [
        (
            conv_buf[0],
            own_cells(shifted, 0, mid, chan),
            [(rows + 1, 0), (1, 2)],
            [0, 1],
            0,
        ),
        (
            conv_buf[1],
            own_cells(shifted, 5, mid, chan),
            [(rows - 5, rows - 4), (rows - 3, rows - 2)],
            [4, 5],
            2,
        ),
        (
            last_buf[...],
            [field[first_row + 3 + h, start : start + SPAN].astype(BF16) for h in range(2)],
            [(rows - 1, rows)],
            [6],
            4,
        ),
    ]
    cells(streams, refs, norm_buf, coarse_in, average)
    load_coarse.wait()
    out_buf[:2] = coarse_rows(coarse_in, 0, 2, coarse_w, coarse_b)
    out_buf[2:5] = coarse_rows(coarse_in, 3, 3, coarse_w, coarse_b)
    count = whole.shape[0]
    low_copy = pltpu.make_async_copy(out_buf.at[:2], whole.at[:2], sems.at[0])
    high_copy = pltpu.make_async_copy(out_buf.at[2:5], whole.at[count - 3 : count], sems.at[1])
    low_copy.start()
    high_copy.start()
    low_copy.wait()
    high_copy.wait()


def local(
    features,
    land_mask,
    dw_weight,
    dw_bias,
    norm_gain,
    norm_shift,
    expand_weight,
    expand_bias,
    project_weight,
    project_bias,
    layer_scale,
    out_gain,
    out_shift,
    coarse_weight,
    coarse_bias,
):
    rows, cols, chan = features.shape
    n_lat = lax.axis_size("lat")
    n_lon = lax.axis_size("lon")
    marks = land_mask.astype(BF16)
    extra = marks.reshape(rows // RIM, RIM, cols)
    around = [(i, (i + 1) % n_lon) for i in range(n_lon)]
    back = [(j, i) for i, j in around]
    to_east = jnp.concatenate([features[:, cols - RIM :], extra], axis=0)
    to_west = jnp.concatenate([features[:, :RIM], extra], axis=0)
    west = lax.ppermute(to_east, "lon", around)
    east = lax.ppermute(to_west, "lon", back)
    lat = jnp.stack([lax.axis_index("lat"), jnp.int32(n_lat - 1)])
    last = rows // 8 - 1
    scalars = pl.BlockSpec(memory_space=pltpu.SMEM)
    vmem = pl.BlockSpec(memory_space=pltpu.VMEM)
    hbm = pl.BlockSpec(memory_space=pl.ANY)
    band = jax.ShapeDtypeStruct((RIM + 1, SPAN, chan), BF16)
    swap_a, swap_b = pl.pallas_call(
        rim_kernel,
        out_shape=(band, band),
        in_specs=[scalars] + [vmem] * 5,
        out_specs=(vmem, vmem),
        scratch_shapes=[pltpu.VMEM((RIM + 1, SPAN, chan), F32)],
        compiler_params=pltpu.CompilerParams(vmem_limit_bytes=8000 * 1024),
        name="rims",
    )(lat, features[:RIM], features[rows - RIM :], west, east, land_mask)
    pairs_a = [(i ^ 1, i) for i in range(n_lat)]
    pairs_b = []
    for i in range(n_lat):
        for j in range(n_lon):
            if i == 0:
                to = (0, j)
            elif i == n_lat - 1:
                to = (i, n_lon - 1 - j)
            else:
                to = (((i + 1) ^ 1) - 1, j)
            pairs_b.append((i * n_lon + j, to[0] * n_lon + to[1]))
    rim_a = lax.ppermute(swap_a, "lat", pairs_a)
    rim_b = lax.ppermute(swap_b, ("lat", "lon"), pairs_b)

    hid = expand_weight.shape[1]
    out_count = coarse_weight.shape[3]
    half_cols = cols // 2
    whole_shape = jax.ShapeDtypeStruct((rows // 2, half_cols, out_count), BF16)
    inner_pairs = rows // 2 - GROUP
    norm_gain, norm_shift, expand_bias, project_bias, layer_scale = (
        v[None] for v in (norm_gain, norm_shift, expand_bias, project_bias, layer_scale)
    )
    out_gain, out_shift, coarse_bias, dw_bias = (
        v[None] for v in (out_gain, out_shift, coarse_bias, dw_bias)
    )
    taps_shape = jax.ShapeDtypeStruct((2 * chan, SIZE * 8 * chan), BF16)
    taps, project = pl.pallas_call(
        prepare_kernel,
        out_shape=(taps_shape, jax.ShapeDtypeStruct((hid + chan, chan), BF16)),
        in_specs=[vmem] * 3,
        out_specs=(hbm, vmem),
        scratch_shapes=[
            pltpu.VMEM(taps_shape.shape, BF16),
            pltpu.SemaphoreType.DMA((4,)),
        ],
        compiler_params=pltpu.CompilerParams(vmem_limit_bytes=58 * 1024 * 1024),
        cost_estimate=pl.CostEstimate(
            flops=2_000_000_000, bytes_accessed=4_000_000, transcendentals=0
        ),
        name="prepare",
    )(dw_weight, project_weight, layer_scale)
    operands = (
        features,
        west,
        east,
        land_mask,
        dw_bias,
        norm_gain,
        norm_shift,
        expand_weight,
        expand_bias,
        project,
        project_bias,
        layer_scale,
        out_gain,
        out_shift,
        coarse_bias,
        taps,
        coarse_weight,
    )
    whole, edges = pl.pallas_call(
        inner_kernel,
        out_shape=(whole_shape, jax.ShapeDtypeStruct((2, half_cols, 8 * chan), BF16)),
        in_specs=[vmem] * (len(operands) - 2) + [hbm] * 2,
        out_specs=(vmem,) * 2,
        scratch_shapes=[
            pltpu.VMEM((rows, SPAN + 16, chan), F32),
            pltpu.VMEM((inner_pairs + 3, SPAN, SIZE * 2 * chan), BF16),
            pltpu.VMEM((GROUP, 2, SPAN, chan), F32),
            pltpu.VMEM((inner_pairs, half_cols, 8 * chan), BF16),
            pltpu.VMEM((SPAN, chan), F32),
            pltpu.VMEM((1, chan), F32),
            pltpu.VMEM((2, 2 * SPAN, 2 * chan), F32),
            pltpu.VMEM(taps_shape.shape, BF16),
            pltpu.VMEM(coarse_weight.shape, BF16),
            pltpu.SemaphoreType.DMA((2,)),
        ],
        compiler_params=pltpu.CompilerParams(vmem_limit_bytes=58 * 1024 * 1024),
        cost_estimate=pl.CostEstimate(
            flops=16_000_000_000, bytes_accessed=8_000_000, transcendentals=0
        ),
        name="inner",
    )(*operands)

    operands = (
        lat,
        features,
        features,
        west,
        east,
        rim_a,
        rim_b,
        land_mask,
        dw_weight,
        dw_bias,
        norm_gain,
        norm_shift,
        expand_weight,
        expand_bias,
        project_bias,
        layer_scale,
        out_gain,
        out_shift,
        coarse_bias,
        project,
        taps,
        edges,
        coarse_weight,
        whole,
    )
    specs = [vmem] * (len(operands) - 4) + [hbm] * 4
    specs[0] = scalars
    specs[1] = pl.BlockSpec((8, cols, chan), lambda i: (0, 0, 0))
    specs[2] = pl.BlockSpec((8, cols, chan), lambda i: (last, 0, 0))
    return pl.pallas_call(
        outer_kernel,
        out_shape=whole_shape,
        grid=(1,),
        in_specs=specs,
        out_specs=hbm,
        scratch_shapes=[
            pltpu.VMEM((24, SPAN + 16, chan), F32),
            pltpu.VMEM((10, SPAN, SIZE * 2 * chan), BF16),
            pltpu.VMEM((SPAN, 2 * chan), F32),
            pltpu.VMEM((5, 2, SPAN, chan), F32),
            pltpu.VMEM((7, half_cols, 8 * chan), BF16),
            pltpu.VMEM((SPAN, chan), F32),
            pltpu.VMEM(taps_shape.shape, BF16),
            pltpu.VMEM(coarse_weight.shape, BF16),
            pltpu.VMEM((2, half_cols, 8 * chan), BF16),
            pltpu.VMEM((1, chan), F32),
            pltpu.VMEM((5, half_cols, out_count), BF16),
            pltpu.VMEM((2, 2 * SPAN, 2 * chan), F32),
            pltpu.SemaphoreType.DMA((3,)),
        ],
        input_output_aliases={len(operands) - 1: 0},
        compiler_params=pltpu.CompilerParams(vmem_limit_bytes=64700 * 1024),
        name="outer",
    )(*operands)


def solution(mesh):
    placed = (
        P("lat", "lon", None),
        P("lat", "lon"),
    ) + (P(),) * 13
    return jax.shard_map(
        local, mesh=mesh, in_specs=placed, out_specs=P("lat", "lon", None), check_vma=False
    )
```

```python
import jax
import jax.numpy as jnp
from jax import lax
from jax.experimental import pallas as pl
from jax.experimental.pallas import tpu as pltpu
from jax.sharding import PartitionSpec as P


F32 = jnp.float32
BF16 = jnp.bfloat16
RIM = 4
LEFT = 8
SIZE = 7
SPAN = 144
GROUP = 4


def dot(a, b):
    return jnp.dot(a, b, preferred_element_type=F32)


def spread_rows(field, shifted, count, chan):
    @pl.loop(0, count)
    def _(p):
        for b in range(SIZE):
            for g in range(2):
                lane = (2 * b + g) * chan
                start = b + LEFT - RIM
                shifted[p, :, lane : lane + chan] = field[2 * p + g, start : start + SPAN].astype(
                    BF16
                )


def centring(chan):
    square = (chan, chan)
    same = lax.broadcasted_iota(jnp.int32, square, 0) == lax.broadcasted_iota(jnp.int32, square, 1)
    return jnp.where(same, F32(1.0), F32(0.0)) - F32(1.0 / chan)


def build_taps(dw, taps, finished):
    chan = dw.shape[2]
    matrix = centring(chan)
    nothing = jnp.zeros((chan, chan), BF16)
    for a in range(-1, SIZE + 1):
        for b in range(SIZE):
            if 0 <= a < SIZE:
                block = (matrix * dw[a, b : b + 1]).astype(BF16)
            else:
                block = nothing
            for h in range(2):
                k, g = divmod(a + h, 2)
                if 0 <= a + h <= SIZE:
                    place = ((k * SIZE + b) * 2 + g) * chan
                    taps[h * chan : (h + 1) * chan, place : place + chan] = block
        if a >= 0 and a % 2 == 1:
            finished(a // 2)


def conv(shifted, starts, taps):
    chan2 = taps.shape[0]
    rhs = taps[...]
    totals = []
    for start in starts:
        lhs = [
            shifted[pl.ds(start + k, 2)].reshape(2 * SPAN, SIZE * chan2) for k in range(4)
        ]
        totals.append(
            lax.dot_general(
                jnp.concatenate(lhs, axis=1),
                rhs,
                (((1,), (1,)), ((), ())),
                preferred_element_type=F32,
            )
        )
    return totals


def average_of(chan):
    both = (2 * chan, 2 * chan)
    row_id = lax.broadcasted_iota(jnp.int32, both, 0)
    col_id = lax.broadcasted_iota(jnp.int32, both, 1)
    return jnp.where(
        (row_id < chan) == (col_id < chan), F32(1.0 / chan), F32(0.0)
    ).astype(BF16)


def two(vector):
    return jnp.concatenate([vector, vector], axis=1)


def centred_row(vector):
    return vector - jnp.mean(vector, axis=-1, keepdims=True)


def cells(streams, refs, norm_buf, coarse_in, average):
    chan = average.shape[0] // 2
    marks, norm_gain, norm_shift, expand, expand_bias, project, project_bias, out_gain, out_shift = refs
    half = coarse_in.shape[1]
    mark_row = lax.broadcasted_iota(jnp.int32, (chan, chan), 0)
    table = marks[...].astype(BF16)
    centred = [s[0] for s in streams]
    spread = [dot((c * c).astype(BF16), average) for c in centred]
    gain, shift = two(norm_gain[...]), two(norm_shift[...])
    normed = [
        (c * lax.rsqrt(v + 1e-06) * gain + shift).astype(BF16) for c, v in zip(centred, spread)
    ]
    parts = [[] for _ in streams]
    for h in range(2):
        for i, s in enumerate(streams):
            pre = dot(normed[i][:, h * chan : (h + 1) * chan], expand[...]) + expand_bias[...]
            hidden = (pre * (1.0 + lax.erf(pre * (0.5**0.5)))).astype(BF16)
            parts[i].append(dot(jnp.concatenate([hidden, s[1][h]], axis=1), project[...]))
    bias = two(project_bias[...])
    updated = [jnp.concatenate(p, axis=1) + bias for p in parts]
    spread = [dot((u * u).astype(BF16), average) for u in updated]
    gain, shift = two(out_gain[...]), two(out_shift[...])
    for i, s in enumerate(streams):
        mark = []
        for rows_of in s[2]:
            chosen = jnp.concatenate(
                [(mark_row == r).astype(F32).astype(BF16) for r in rows_of], axis=1
            )
            mark.append(dot(table, chosen))
        mark = jnp.concatenate(mark, axis=0)
        normalized = mark * (updated[i] * lax.rsqrt(spread[i] + 1e-06) * gain + shift)
        for j, slot in enumerate(s[3]):
            for h in range(2):
                buf = norm_buf.at[s[4] + j, h]
                buf[...] = normalized[j * SPAN : (j + 1) * SPAN, h * chan : (h + 1) * chan]
                for b in range(4):
                    lane = (2 * b + h) * chan
                    coarse_in[slot, :, lane : lane + chan] = buf[
                        pl.ds(b, half, stride=2), :
                    ].astype(BF16)


def coarse_rows(coarse_in, bands, coarse_w, coarse_b):
    kernel = jnp.concatenate(
        [coarse_w[2 * k + h, b] for k in range(2) for b in range(4) for h in range(2)], axis=0
    )
    windows = []
    for first, count in bands:
        rows = [coarse_in[first + k : first + k + count] for k in range(2)]
        windows.append(jnp.concatenate(rows, axis=2))
    window = jnp.concatenate(windows, axis=0)
    total = dot(window.reshape(-1, window.shape[2]), kernel) + coarse_b[...]
    return total.astype(BF16).reshape(window.shape[0], coarse_in.shape[1], -1)


def own_cells(shifted, at, mid, chan):
    return [
        shifted[
            pl.ds(at + 1 + h, 2), :, mid + (1 - h) * chan : mid + (2 - h) * chan
        ].reshape(2 * SPAN, chan)
        for h in range(2)
    ]


def inner_kernel(
    feat,
    west,
    east,
    land_mask,
    dw,
    dw_bias,
    norm_gain,
    norm_shift,
    expand,
    expand_bias,
    project_w,
    project_b,
    layer_scale,
    out_gain,
    out_shift,
    coarse_b,
    coarse_w_hbm,
    out,
    edges,
    project,
    taps_hbm,
    field,
    shifted,
    norm_buf,
    coarse_in,
    marks,
    project_bias,
    conv_buf,
    taps,
    coarse_w,
    sems,
):
    rows, cols, chan = feat.shape
    depth = taps.shape[1] // 4

    def piece(k):
        cut = slice(k * depth, (k + 1) * depth)
        return pltpu.make_async_copy(taps.at[:, cut], taps_hbm.at[:, cut], sems.at[k])

    load_coarse = pltpu.make_async_copy(coarse_w_hbm, coarse_w, sems.at[4])
    load_coarse.start()
    build_taps(dw, taps, lambda k: piece(k).start())
    hid = project_w.shape[0]
    scaled = project_w[...].astype(F32) * layer_scale[...]
    project[:hid] = (0.5 * centred_row(scaled)).astype(BF16)
    project[hid:] = centring(chan).astype(BF16)
    field[:, : LEFT - RIM] = jnp.zeros((rows, LEFT - RIM, chan), F32)
    field[:, LEFT + cols + RIM :] = jnp.zeros((rows, SPAN + 16 - LEFT - cols - RIM, chan), F32)
    field[:, LEFT : LEFT + cols] = feat[...].astype(F32)
    field[:, LEFT - RIM : LEFT] = west[:rows].astype(F32)
    field[:, LEFT + cols : LEFT + cols + RIM] = east[:rows].astype(F32)
    count = shifted.shape[0]
    spread_rows(field, shifted, count, chan)

    project_bias[...] = centred_row(project_b[...] * layer_scale[...])

    side_table(land_mask, west, east, marks)
    average = average_of(chan)
    bias = two(centred_row(dw_bias[...]))
    refs = (
        marks,
        norm_gain,
        norm_shift,
        expand,
        expand_bias,
        project,
        project_bias,
        out_gain,
        out_shift,
    )
    mid = (SIZE // 2) * 2 * chan

    @pl.loop(0, (count - 3) // GROUP)
    def _(group):
        base = group * GROUP
        streams = []

        @pl.when(group >= 0)
        def _():
            for i, total in enumerate(conv(shifted, [base, base + 2], taps)):
                conv_buf[i] = total + bias

        for i in range(2):
            slot = base + 2 * i
            top = 2 * (slot + 2)
            streams.append(
                (
                    conv_buf[i],
                    own_cells(shifted, slot, mid, chan),
                    [(top - 1, top), (top + 1, top + 2)],
                    [slot, slot + 1],
                    2 * i,
                )
            )
        cells(streams, refs, norm_buf, coarse_in, average)

    done = coarse_in.shape[0] - 1
    load_coarse.wait()
    out[2 : 2 + done] = coarse_rows(coarse_in, [(0, done)], coarse_w, coarse_b)
    edges[0] = coarse_in[0]
    edges[1] = coarse_in[done]
    for k in range(4):
        piece(k).wait()


def side_table(land_mask, west, east, marks):
    rows, cols = land_mask.shape

    def neighbour(packed):
        lines = [packed[rows + m] for m in range(rows // RIM)]
        return jnp.concatenate([line.astype(F32) for line in lines], axis=0)

    def turned(block):
        return jnp.concatenate([block, jnp.zeros((cols - rows, cols), F32)], axis=0).T

    own = turned(land_mask[...].astype(F32))
    left = turned(neighbour(west))
    right = turned(neighbour(east))
    marks[cols:, :] = jnp.zeros((SPAN - cols, cols), F32)
    marks[1 : cols + 1, :] = own
    marks[0:1, :] = left[cols - 1 : cols]
    marks[cols + 1 : cols + 2, :] = right[0:1]


def rim_kernel(lat, feat_low, feat_high, west, east, land_mask, swap_a, swap_b, block):
    rows, cols = land_mask.shape
    chan = feat_low.shape[2]
    parity = lat[0] % 2
    deep = lax.broadcasted_iota(jnp.int32, (SPAN, cols), 1)
    place = lax.broadcasted_iota(jnp.int32, (SPAN, cols), 0)
    ones = jnp.ones((cols, chan), BF16)

    def fill(feat, first, row):
        block[:RIM, RIM : RIM + cols] = feat[...].astype(F32)
        block[:RIM, :RIM] = west[first : first + RIM].astype(F32)
        block[:RIM, RIM + cols : 2 * RIM + cols] = east[first : first + RIM].astype(F32)
        block[:RIM, 2 * RIM + cols :] = jnp.zeros((RIM, SPAN - 2 * RIM - cols, chan), F32)
        at, part = divmod(row, RIM)
        left = west[rows + at].astype(F32)[part : part + 1]
        right = east[rows + at].astype(F32)[part : part + 1]
        line = land_mask[...].astype(F32)[row : row + 1]
        zero = jnp.zeros((SPAN, cols), F32)
        table = (
            jnp.where(deep == place - RIM, line, zero)
            + jnp.where((place == RIM - 1) & (deep == cols - 1), left, zero)
            + jnp.where((place == RIM + cols) & (deep == 0), right, zero)
        )
        block[RIM] = dot(table.astype(BF16), ones)

    fill(feat_high, rows - RIM, rows - 1)

    @pl.when(parity == 0)
    def _():
        swap_a[...] = block[...].astype(BF16)

    @pl.when(parity == 1)
    def _():
        swap_b[...] = block[...].astype(BF16)

    @pl.when(lat[0] == lat[1])
    def _():
        width = cols + 2 * RIM
        wide = (SPAN, SPAN)
        total = lax.broadcasted_iota(jnp.int32, wide, 0) + lax.broadcasted_iota(jnp.int32, wide, 1)
        turn = (total == width - 1).astype(F32).astype(BF16)
        for r in range(RIM + 1):
            source = RIM - 1 - r if r < RIM else r
            swap_b[r] = dot(turn, block[source].astype(BF16)).astype(BF16)

    fill(feat_low, 0, 0)

    @pl.when(parity == 0)
    def _():
        swap_b[...] = block[...].astype(BF16)

    @pl.when(parity == 1)
    def _():
        swap_a[...] = block[...].astype(BF16)


def outer_kernel(
    lat,
    feat_low,
    feat_high,
    west,
    east,
    rim_a,
    rim_b,
    land_mask,
    dw,
    dw_bias,
    norm_gain,
    norm_shift,
    expand,
    expand_bias,
    project_b,
    layer_scale,
    out_gain,
    out_shift,
    coarse_b,
    project,
    taps_hbm,
    edges_hbm,
    coarse_w_hbm,
    whole_in,
    whole,
    field,
    shifted,
    last_buf,
    norm_buf,
    coarse_in,
    marks,
    taps,
    coarse_w,
    edges,
    project_bias,
    out_buf,
    conv_buf,
    sems,
):
    del whole_in
    load_taps = pltpu.make_async_copy(taps_hbm, taps, sems.at[0])
    load_edges = pltpu.make_async_copy(edges_hbm, edges, sems.at[2])
    load_coarse = pltpu.make_async_copy(coarse_w_hbm, coarse_w, sems.at[1])
    load_taps.start()
    load_edges.start()
    load_coarse.start()
    project_bias[...] = centred_row(project_b[...] * layer_scale[...])
    chan = feat_low.shape[2]
    rows, cols = land_mask.shape
    low = 6
    high = RIM + low
    top = high + 8
    used = top + RIM
    left, right = LEFT - RIM, LEFT + cols + RIM
    field[:, :left] = jnp.zeros((used + 2, left, chan), F32)
    field[:, right:] = jnp.zeros((used + 2, SPAN + 16 - right, chan), F32)

    def place(south, north):
        field[:RIM, left:right] = south[:RIM, : right - left].astype(F32)
        field[top:used, left:right] = north[:RIM, : right - left].astype(F32)
        field[used, left:right] = north[RIM, : right - left].astype(F32)
        field[used + 1, left:right] = south[RIM, : right - left].astype(F32)

    @pl.when(lat[0] % 2 == 0)
    def _():
        place(rim_b, rim_a)

    @pl.when(lat[0] % 2 == 1)
    def _():
        place(rim_a, rim_b)

    @pl.when(lat[0] == 0)
    def _():
        field[:RIM, left:right] = jnp.zeros((RIM, right - left, chan), F32)
        field[used + 1, left:right] = jnp.zeros((right - left, chan), F32)

    field[RIM:high, LEFT : LEFT + cols] = feat_low[:low].astype(F32)
    field[RIM:high, left:LEFT] = west[:low].astype(F32)
    field[RIM:high, LEFT + cols : right] = east[:low].astype(F32)
    field[high:top, LEFT : LEFT + cols] = feat_high[...].astype(F32)
    field[high:top, left:LEFT] = west[rows - 8 : rows].astype(F32)
    field[high:top, LEFT + cols : right] = east[rows - 8 : rows].astype(F32)

    side_table(land_mask, west, east, marks)
    lane = lax.broadcasted_iota(jnp.int32, (SPAN, chan), 1)
    start = LEFT - 1
    table = jnp.where(lane == rows, field[used, start : start + SPAN], marks[...])
    marks[...] = jnp.where(lane == rows + 1, field[used + 1, start : start + SPAN], table)
    spread_rows(field, shifted, shifted.shape[0], chan)

    average = average_of(chan)
    bias = two(centred_row(dw_bias[...]))
    refs = (
        marks,
        norm_gain,
        norm_shift,
        expand,
        expand_bias,
        project,
        project_bias,
        out_gain,
        out_shift,
    )
    mid = (SIZE // 2) * 2 * chan
    part = SPAN // 2
    first_row = high + 4
    turned = lat[0] == lat[1]
    for n in range(0, SPAN, part):
        accs = [jnp.zeros((part, chan), F32) + dw_bias[...] for _ in range(2)]
        for r in range(SIZE + 1):
            for b in range(SIZE):
                start = n + b + left
                piece = field[first_row + r, start : start + part]
                if r < SIZE:
                    accs[0] = accs[0] + piece * dw[r, b : b + 1]
                if r > 0:
                    weight = jnp.where(
                        turned,
                        dw[SIZE - r, SIZE - 1 - b : SIZE - b],
                        dw[r - 1, b : b + 1],
                    )
                    accs[1] = accs[1] + piece * weight
        for h in range(2):
            last_buf[n : n + part, h * chan : (h + 1) * chan] = centred_row(accs[h])

    load_taps.wait()
    load_edges.wait()
    coarse_in[2] = edges[0]
    coarse_in[3] = edges[1]

    @pl.when(lat[0] >= 0)
    def _():
        for i, total in enumerate(conv(shifted, [0, 5], taps)):
            conv_buf[i] = total + bias

    start = SIZE // 2 + left
    streams = [
        (
            conv_buf[0],
            own_cells(shifted, 0, mid, chan),
            [(rows + 1, 0), (1, 2)],
            [0, 1],
            0,
        ),
        (
            conv_buf[1],
            own_cells(shifted, 5, mid, chan),
            [(rows - 5, rows - 4), (rows - 3, rows - 2)],
            [4, 5],
            2,
        ),
        (
            last_buf[...],
            [field[first_row + 3 + h, start : start + SPAN].astype(BF16) for h in range(2)],
            [(rows - 1, rows)],
            [6],
            4,
        ),
    ]
    cells(streams, refs, norm_buf, coarse_in, average)
    load_coarse.wait()
    out_buf[...] = coarse_rows(coarse_in, [(0, 2), (3, 3)], coarse_w, coarse_b)
    count = whole.shape[0]
    low_copy = pltpu.make_async_copy(out_buf.at[:2], whole.at[:2], sems.at[0])
    high_copy = pltpu.make_async_copy(out_buf.at[2:5], whole.at[count - 3 : count], sems.at[1])
    low_copy.start()
    high_copy.start()
    low_copy.wait()
    high_copy.wait()


def local(
    features,
    land_mask,
    dw_weight,
    dw_bias,
    norm_gain,
    norm_shift,
    expand_weight,
    expand_bias,
    project_weight,
    project_bias,
    layer_scale,
    out_gain,
    out_shift,
    coarse_weight,
    coarse_bias,
):
    rows, cols, chan = features.shape
    n_lat = lax.axis_size("lat")
    n_lon = lax.axis_size("lon")
    marks = land_mask.astype(BF16)
    extra = marks.reshape(rows // RIM, RIM, cols)
    around = [(i, (i + 1) % n_lon) for i in range(n_lon)]
    back = [(j, i) for i, j in around]
    to_east = jnp.concatenate([features[:, cols - RIM :], extra], axis=0)
    to_west = jnp.concatenate([features[:, :RIM], extra], axis=0)
    west = lax.ppermute(to_east, "lon", around)
    east = lax.ppermute(to_west, "lon", back)
    lat = jnp.stack([lax.axis_index("lat"), jnp.int32(n_lat - 1)])
    last = rows // 8 - 1
    scalars = pl.BlockSpec(memory_space=pltpu.SMEM)
    vmem = pl.BlockSpec(memory_space=pltpu.VMEM)
    hbm = pl.BlockSpec(memory_space=pl.ANY)
    band = jax.ShapeDtypeStruct((RIM + 1, SPAN, chan), BF16)
    swap_a, swap_b = pl.pallas_call(
        rim_kernel,
        out_shape=(band, band),
        in_specs=[scalars] + [vmem] * 5,
        out_specs=(vmem, vmem),
        scratch_shapes=[pltpu.VMEM((RIM + 1, SPAN, chan), F32)],
        compiler_params=pltpu.CompilerParams(vmem_limit_bytes=8000 * 1024),
        name="rims",
    )(lat, features[:RIM], features[rows - RIM :], west, east, marks)
    pairs_a = [(i ^ 1, i) for i in range(n_lat)]
    pairs_b = []
    for i in range(n_lat):
        for j in range(n_lon):
            if i == 0:
                to = (0, j)
            elif i == n_lat - 1:
                to = (i, n_lon - 1 - j)
            else:
                to = (((i + 1) ^ 1) - 1, j)
            pairs_b.append((i * n_lon + j, to[0] * n_lon + to[1]))
    rim_a = lax.ppermute(swap_a, "lat", pairs_a)
    rim_b = lax.ppermute(swap_b, ("lat", "lon"), pairs_b)

    hid = expand_weight.shape[1]
    out_count = coarse_weight.shape[3]
    half_cols = cols // 2
    whole_shape = jax.ShapeDtypeStruct((rows // 2, half_cols, out_count), BF16)
    inner_pairs = rows // 2 - GROUP
    norm_gain, norm_shift, expand_bias, project_bias, layer_scale = (
        v[None] for v in (norm_gain, norm_shift, expand_bias, project_bias, layer_scale)
    )
    out_gain, out_shift, coarse_bias, dw_bias = (
        v[None] for v in (out_gain, out_shift, coarse_bias, dw_bias)
    )
    taps_shape = jax.ShapeDtypeStruct((2 * chan, SIZE * 8 * chan), BF16)
    operands = (
        features,
        west,
        east,
        land_mask,
        dw_weight,
        dw_bias,
        norm_gain,
        norm_shift,
        expand_weight,
        expand_bias,
        project_weight,
        project_bias,
        layer_scale,
        out_gain,
        out_shift,
        coarse_bias,
        coarse_weight,
    )
    whole, edges, project, taps = pl.pallas_call(
        inner_kernel,
        out_shape=(
            whole_shape,
            jax.ShapeDtypeStruct((2, half_cols, 8 * chan), BF16),
            jax.ShapeDtypeStruct((hid + chan, chan), BF16),
            taps_shape,
        ),
        in_specs=[vmem] * (len(operands) - 1) + [hbm],
        out_specs=(vmem, vmem, vmem, hbm),
        scratch_shapes=[
            pltpu.VMEM((rows, SPAN + 16, chan), F32),
            pltpu.VMEM((inner_pairs + 3, SPAN, SIZE * 2 * chan), BF16),
            pltpu.VMEM((GROUP, 2, SPAN, chan), F32),
            pltpu.VMEM((inner_pairs, half_cols, 8 * chan), BF16),
            pltpu.VMEM((SPAN, chan), F32),
            pltpu.VMEM((1, chan), F32),
            pltpu.VMEM((2, 2 * SPAN, 2 * chan), F32),
            pltpu.VMEM(taps_shape.shape, BF16),
            pltpu.VMEM(coarse_weight.shape, BF16),
            pltpu.SemaphoreType.DMA((5,)),
        ],
        compiler_params=pltpu.CompilerParams(vmem_limit_bytes=58 * 1024 * 1024),
        cost_estimate=pl.CostEstimate(
            flops=16_000_000_000, bytes_accessed=8_000_000, transcendentals=0
        ),
        name="inner",
    )(*operands)

    operands = (
        lat,
        features,
        features,
        west,
        east,
        rim_a,
        rim_b,
        land_mask,
        dw_weight,
        dw_bias,
        norm_gain,
        norm_shift,
        expand_weight,
        expand_bias,
        project_bias,
        layer_scale,
        out_gain,
        out_shift,
        coarse_bias,
        project,
        taps,
        edges,
        coarse_weight,
        whole,
    )
    specs = [vmem] * (len(operands) - 4) + [hbm] * 4
    specs[0] = scalars
    specs[1] = pl.BlockSpec((8, cols, chan), lambda i: (0, 0, 0))
    specs[2] = pl.BlockSpec((8, cols, chan), lambda i: (last, 0, 0))
    return pl.pallas_call(
        outer_kernel,
        out_shape=whole_shape,
        grid=(1,),
        in_specs=specs,
        out_specs=hbm,
        scratch_shapes=[
            pltpu.VMEM((24, SPAN + 16, chan), F32),
            pltpu.VMEM((10, SPAN, SIZE * 2 * chan), BF16),
            pltpu.VMEM((SPAN, 2 * chan), F32),
            pltpu.VMEM((5, 2, SPAN, chan), F32),
            pltpu.VMEM((7, half_cols, 8 * chan), BF16),
            pltpu.VMEM((SPAN, chan), F32),
            pltpu.VMEM(taps_shape.shape, BF16),
            pltpu.VMEM(coarse_weight.shape, BF16),
            pltpu.VMEM((2, half_cols, 8 * chan), BF16),
            pltpu.VMEM((1, chan), F32),
            pltpu.VMEM((5, half_cols, out_count), BF16),
            pltpu.VMEM((2, 2 * SPAN, 2 * chan), F32),
            pltpu.SemaphoreType.DMA((3,)),
        ],
        input_output_aliases={len(operands) - 1: 0},
        compiler_params=pltpu.CompilerParams(vmem_limit_bytes=64700 * 1024),
        name="outer",
    )(*operands)


def solution(mesh):
    placed = (
        P("lat", "lon", None),
        P("lat", "lon"),
    ) + (P(),) * 13
    return jax.shard_map(
        local, mesh=mesh, in_specs=placed, out_specs=P("lat", "lon", None), check_vma=False
    )
```

```python
import jax
import jax.numpy as jnp
from jax import lax
from jax.experimental import pallas as pl
from jax.experimental.pallas import tpu as pltpu
from jax.sharding import PartitionSpec as P


F32 = jnp.float32
BF16 = jnp.bfloat16
RIM = 4
LEFT = 8
SIZE = 7
SPAN = 144
GROUP = 4


def dot(a, b):
    return jnp.dot(a, b, preferred_element_type=F32)


def spread_rows(field, shifted, count, chan):
    @pl.loop(0, count)
    def _(p):
        for b in range(SIZE):
            for g in range(2):
                lane = (2 * b + g) * chan
                start = b + LEFT - RIM
                shifted[p, :, lane : lane + chan] = field[2 * p + g, start : start + SPAN].astype(
                    BF16
                )


def centring(chan):
    square = (chan, chan)
    same = lax.broadcasted_iota(jnp.int32, square, 0) == lax.broadcasted_iota(jnp.int32, square, 1)
    return jnp.where(same, F32(1.0), F32(0.0)) - F32(1.0 / chan)


def build_taps(dw, taps, finished):
    chan = dw.shape[2]
    matrix = centring(chan)
    nothing = jnp.zeros((chan, chan), BF16)
    for a in range(-1, SIZE + 1):
        for b in range(SIZE):
            if 0 <= a < SIZE:
                block = (matrix * dw[a, b : b + 1]).astype(BF16)
            else:
                block = nothing
            for h in range(2):
                k, g = divmod(a + h, 2)
                if 0 <= a + h <= SIZE:
                    place = ((k * SIZE + b) * 2 + g) * chan
                    taps[h * chan : (h + 1) * chan, place : place + chan] = block
        if a >= 0 and a % 2 == 1:
            finished(a // 2)


def conv(shifted, starts, taps):
    chan2 = taps.shape[0]
    rhs = taps[...]
    totals = []
    for start in starts:
        lhs = [
            shifted[pl.ds(start + k, 2)].reshape(2 * SPAN, SIZE * chan2) for k in range(4)
        ]
        totals.append(
            lax.dot_general(
                jnp.concatenate(lhs, axis=1),
                rhs,
                (((1,), (1,)), ((), ())),
                preferred_element_type=F32,
            )
        )
    return totals


def average_of(chan):
    both = (2 * chan, 2 * chan)
    row_id = lax.broadcasted_iota(jnp.int32, both, 0)
    col_id = lax.broadcasted_iota(jnp.int32, both, 1)
    return jnp.where(
        (row_id < chan) == (col_id < chan), F32(1.0 / chan), F32(0.0)
    ).astype(BF16)


def two(vector):
    return jnp.concatenate([vector, vector], axis=1)


def centred_row(vector):
    return vector - jnp.mean(vector, axis=-1, keepdims=True)


def cells(streams, refs, norm_buf, coarse_in, average):
    chan = average.shape[0] // 2
    marks, norm_gain, norm_shift, expand, expand_bias, project, project_bias, out_gain, out_shift = refs
    half = coarse_in.shape[1]
    mark_row = lax.broadcasted_iota(jnp.int32, (chan, chan), 0)
    table = marks[...].astype(BF16)
    centred = [s[0] for s in streams]
    spread = [dot((c * c).astype(BF16), average) for c in centred]
    gain, shift = two(norm_gain[...]), two(norm_shift[...])
    normed = [
        (c * lax.rsqrt(v + 1e-06) * gain + shift).astype(BF16) for c, v in zip(centred, spread)
    ]
    parts = [[] for _ in streams]
    for h in range(2):
        for i, s in enumerate(streams):
            pre = dot(normed[i][:, h * chan : (h + 1) * chan], expand[...]) + expand_bias[...]
            hidden = (pre * (1.0 + lax.erf(pre * (0.5**0.5)))).astype(BF16)
            parts[i].append(dot(jnp.concatenate([hidden, s[1][h]], axis=1), project[...]))
    bias = two(project_bias[...])
    updated = [jnp.concatenate(p, axis=1) + bias for p in parts]
    spread = [dot((u * u).astype(BF16), average) for u in updated]
    gain, shift = two(out_gain[...]), two(out_shift[...])
    for i, s in enumerate(streams):
        mark = []
        for rows_of in s[2]:
            chosen = jnp.concatenate(
                [(mark_row == r).astype(F32).astype(BF16) for r in rows_of], axis=1
            )
            mark.append(dot(table, chosen))
        mark = jnp.concatenate(mark, axis=0)
        normalized = mark * (updated[i] * lax.rsqrt(spread[i] + 1e-06) * gain + shift)
        for j, slot in enumerate(s[3]):
            for h in range(2):
                buf = norm_buf.at[s[4] + j, h]
                buf[...] = normalized[j * SPAN : (j + 1) * SPAN, h * chan : (h + 1) * chan]
                for b in range(4):
                    lane = (2 * b + h) * chan
                    coarse_in[slot, :, lane : lane + chan] = buf[
                        pl.ds(b, half, stride=2), :
                    ].astype(BF16)


def coarse_rows(coarse_in, bands, coarse_w, coarse_b):
    kernel = jnp.concatenate(
        [coarse_w[2 * k + h, b] for k in range(2) for b in range(4) for h in range(2)], axis=0
    )
    windows = []
    for first, count in bands:
        rows = [coarse_in[first + k : first + k + count] for k in range(2)]
        windows.append(jnp.concatenate(rows, axis=2))
    window = jnp.concatenate(windows, axis=0)
    total = dot(window.reshape(-1, window.shape[2]), kernel) + coarse_b[...]
    return total.astype(BF16).reshape(window.shape[0], coarse_in.shape[1], -1)


def own_cells(shifted, at, mid, chan):
    return [
        shifted[
            pl.ds(at + 1 + h, 2), :, mid + (1 - h) * chan : mid + (2 - h) * chan
        ].reshape(2 * SPAN, chan)
        for h in range(2)
    ]


def inner_kernel(
    feat,
    west,
    east,
    land_mask,
    dw,
    dw_bias,
    norm_gain,
    norm_shift,
    expand,
    expand_bias,
    project_w,
    project_b,
    layer_scale,
    out_gain,
    out_shift,
    coarse_b,
    coarse_w_hbm,
    out,
    edges,
    project,
    taps_hbm,
    field,
    shifted,
    norm_buf,
    coarse_in,
    marks,
    project_bias,
    conv_buf,
    taps,
    coarse_w,
    sems,
):
    rows, cols, chan = feat.shape
    depth = taps.shape[1] // 4

    def piece(k):
        cut = slice(k * depth, (k + 1) * depth)
        return pltpu.make_async_copy(taps.at[:, cut], taps_hbm.at[:, cut], sems.at[k])

    load_coarse = pltpu.make_async_copy(coarse_w_hbm, coarse_w, sems.at[4])
    load_coarse.start()
    build_taps(dw, taps, lambda k: piece(k).start())
    hid = project_w.shape[0]
    scaled = project_w[...].astype(F32) * layer_scale[...]
    project[:hid] = (0.5 * centred_row(scaled)).astype(BF16)
    project[hid:] = centring(chan).astype(BF16)
    field[:, : LEFT - RIM] = jnp.zeros((rows, LEFT - RIM, chan), F32)
    field[:, LEFT + cols + RIM :] = jnp.zeros((rows, SPAN + 16 - LEFT - cols - RIM, chan), F32)
    field[:, LEFT : LEFT + cols] = feat[...].astype(F32)
    field[:, LEFT - RIM : LEFT] = west[:rows].astype(F32)
    field[:, LEFT + cols : LEFT + cols + RIM] = east[:rows].astype(F32)
    count = shifted.shape[0]
    spread_rows(field, shifted, count, chan)

    project_bias[...] = centred_row(project_b[...] * layer_scale[...])

    side_table(land_mask, west, east, marks)
    average = average_of(chan)
    bias = two(centred_row(dw_bias[...]))
    refs = (
        marks,
        norm_gain,
        norm_shift,
        expand,
        expand_bias,
        project,
        project_bias,
        out_gain,
        out_shift,
    )
    mid = (SIZE // 2) * 2 * chan

    @pl.loop(0, (count - 3) // GROUP)
    def _(group):
        base = group * GROUP
        streams = []

        @pl.when(group >= 0)
        def _():
            for i, total in enumerate(conv(shifted, [base, base + 2], taps)):
                conv_buf[i] = total + bias

        for i in range(2):
            slot = base + 2 * i
            top = 2 * (slot + 2)
            streams.append(
                (
                    conv_buf[i],
                    own_cells(shifted, slot, mid, chan),
                    [(top - 1, top), (top + 1, top + 2)],
                    [slot, slot + 1],
                    2 * i,
                )
            )
        cells(streams, refs, norm_buf, coarse_in, average)

    done = coarse_in.shape[0] - 1
    load_coarse.wait()
    out[2 : 2 + done] = coarse_rows(coarse_in, [(0, done)], coarse_w, coarse_b)
    edges[0] = coarse_in[0]
    edges[1] = coarse_in[done]
    for k in range(4):
        piece(k).wait()


def side_table(land_mask, west, east, marks):
    rows, cols = land_mask.shape

    def neighbour(packed):
        lines = [packed[rows + m] for m in range(rows // RIM)]
        return jnp.concatenate([line.astype(F32) for line in lines], axis=0)

    def turned(block):
        return jnp.concatenate([block, jnp.zeros((cols - rows, cols), F32)], axis=0).T

    own = turned(land_mask[...].astype(F32))
    left = turned(neighbour(west))
    right = turned(neighbour(east))
    marks[cols:, :] = jnp.zeros((SPAN - cols, cols), F32)
    marks[1 : cols + 1, :] = own
    marks[0:1, :] = left[cols - 1 : cols]
    marks[cols + 1 : cols + 2, :] = right[0:1]


def side_kernel(first, last, land_mask, to_west, to_east):
    rows, width, _ = first.shape
    to_west[:rows] = first[...].astype(F32)[:, :RIM].astype(BF16)
    to_east[:rows] = last[...].astype(F32)[:, width - RIM :].astype(BF16)
    mask = land_mask[...].astype(F32)
    for m in range(rows // RIM):
        lines = mask[m * RIM : (m + 1) * RIM].astype(BF16)
        to_west[rows + m] = lines
        to_east[rows + m] = lines


def rim_kernel(lat, feat_low, feat_high, west, east, land_mask, swap_a, swap_b, block):
    rows, cols = land_mask.shape
    chan = feat_low.shape[2]
    parity = lat[0] % 2
    deep = lax.broadcasted_iota(jnp.int32, (SPAN, cols), 1)
    place = lax.broadcasted_iota(jnp.int32, (SPAN, cols), 0)
    ones = jnp.ones((cols, chan), BF16)

    def fill(feat, first, row):
        block[:RIM, RIM : RIM + cols] = feat[...].astype(F32)
        block[:RIM, :RIM] = west[first : first + RIM].astype(F32)
        block[:RIM, RIM + cols : 2 * RIM + cols] = east[first : first + RIM].astype(F32)
        block[:RIM, 2 * RIM + cols :] = jnp.zeros((RIM, SPAN - 2 * RIM - cols, chan), F32)
        at, part = divmod(row, RIM)
        left = west[rows + at].astype(F32)[part : part + 1]
        right = east[rows + at].astype(F32)[part : part + 1]
        line = land_mask[...].astype(F32)[row : row + 1]
        zero = jnp.zeros((SPAN, cols), F32)
        table = (
            jnp.where(deep == place - RIM, line, zero)
            + jnp.where((place == RIM - 1) & (deep == cols - 1), left, zero)
            + jnp.where((place == RIM + cols) & (deep == 0), right, zero)
        )
        block[RIM] = dot(table.astype(BF16), ones)

    fill(feat_high, rows - RIM, rows - 1)

    @pl.when(parity == 0)
    def _():
        swap_a[...] = block[...].astype(BF16)

    @pl.when(parity == 1)
    def _():
        swap_b[...] = block[...].astype(BF16)

    @pl.when(lat[0] == lat[1])
    def _():
        width = cols + 2 * RIM
        wide = (SPAN, SPAN)
        total = lax.broadcasted_iota(jnp.int32, wide, 0) + lax.broadcasted_iota(jnp.int32, wide, 1)
        turn = (total == width - 1).astype(F32).astype(BF16)
        for r in range(RIM + 1):
            source = RIM - 1 - r if r < RIM else r
            swap_b[r] = dot(turn, block[source].astype(BF16)).astype(BF16)

    fill(feat_low, 0, 0)

    @pl.when(parity == 0)
    def _():
        swap_b[...] = block[...].astype(BF16)

    @pl.when(parity == 1)
    def _():
        swap_a[...] = block[...].astype(BF16)


def outer_kernel(
    lat,
    feat_low,
    feat_high,
    west,
    east,
    rim_a,
    rim_b,
    land_mask,
    dw,
    dw_bias,
    norm_gain,
    norm_shift,
    expand,
    expand_bias,
    project_b,
    layer_scale,
    out_gain,
    out_shift,
    coarse_b,
    project,
    taps_hbm,
    edges_hbm,
    coarse_w_hbm,
    whole_in,
    whole,
    field,
    shifted,
    last_buf,
    norm_buf,
    coarse_in,
    marks,
    taps,
    coarse_w,
    edges,
    project_bias,
    out_buf,
    conv_buf,
    sems,
):
    del whole_in
    load_taps = pltpu.make_async_copy(taps_hbm, taps, sems.at[0])
    load_edges = pltpu.make_async_copy(edges_hbm, edges, sems.at[2])
    load_coarse = pltpu.make_async_copy(coarse_w_hbm, coarse_w, sems.at[1])
    load_taps.start()
    load_edges.start()
    load_coarse.start()
    project_bias[...] = centred_row(project_b[...] * layer_scale[...])
    chan = feat_low.shape[2]
    rows, cols = land_mask.shape
    low = 6
    high = RIM + low
    top = high + 8
    used = top + RIM
    left, right = LEFT - RIM, LEFT + cols + RIM
    field[:, :left] = jnp.zeros((used + 2, left, chan), F32)
    field[:, right:] = jnp.zeros((used + 2, SPAN + 16 - right, chan), F32)

    def place(south, north):
        field[:RIM, left:right] = south[:RIM, : right - left].astype(F32)
        field[top:used, left:right] = north[:RIM, : right - left].astype(F32)
        field[used, left:right] = north[RIM, : right - left].astype(F32)
        field[used + 1, left:right] = south[RIM, : right - left].astype(F32)

    @pl.when(lat[0] % 2 == 0)
    def _():
        place(rim_b, rim_a)

    @pl.when(lat[0] % 2 == 1)
    def _():
        place(rim_a, rim_b)

    @pl.when(lat[0] == 0)
    def _():
        field[:RIM, left:right] = jnp.zeros((RIM, right - left, chan), F32)
        field[used + 1, left:right] = jnp.zeros((right - left, chan), F32)

    field[RIM:high, LEFT : LEFT + cols] = feat_low[:low].astype(F32)
    field[RIM:high, left:LEFT] = west[:low].astype(F32)
    field[RIM:high, LEFT + cols : right] = east[:low].astype(F32)
    field[high:top, LEFT : LEFT + cols] = feat_high[...].astype(F32)
    field[high:top, left:LEFT] = west[rows - 8 : rows].astype(F32)
    field[high:top, LEFT + cols : right] = east[rows - 8 : rows].astype(F32)

    side_table(land_mask, west, east, marks)
    lane = lax.broadcasted_iota(jnp.int32, (SPAN, chan), 1)
    start = LEFT - 1
    table = jnp.where(lane == rows, field[used, start : start + SPAN], marks[...])
    marks[...] = jnp.where(lane == rows + 1, field[used + 1, start : start + SPAN], table)
    spread_rows(field, shifted, shifted.shape[0], chan)

    average = average_of(chan)
    bias = two(centred_row(dw_bias[...]))
    refs = (
        marks,
        norm_gain,
        norm_shift,
        expand,
        expand_bias,
        project,
        project_bias,
        out_gain,
        out_shift,
    )
    mid = (SIZE // 2) * 2 * chan
    part = SPAN // 2
    first_row = high + 4
    turned = lat[0] == lat[1]
    for n in range(0, SPAN, part):
        accs = [jnp.zeros((part, chan), F32) + dw_bias[...] for _ in range(2)]
        for r in range(SIZE + 1):
            for b in range(SIZE):
                start = n + b + left
                piece = field[first_row + r, start : start + part]
                if r < SIZE:
                    accs[0] = accs[0] + piece * dw[r, b : b + 1]
                if r > 0:
                    weight = jnp.where(
                        turned,
                        dw[SIZE - r, SIZE - 1 - b : SIZE - b],
                        dw[r - 1, b : b + 1],
                    )
                    accs[1] = accs[1] + piece * weight
        for h in range(2):
            last_buf[n : n + part, h * chan : (h + 1) * chan] = centred_row(accs[h])

    load_taps.wait()
    load_edges.wait()
    coarse_in[2] = edges[0]
    coarse_in[3] = edges[1]

    @pl.when(lat[0] >= 0)
    def _():
        for i, total in enumerate(conv(shifted, [0, 5], taps)):
            conv_buf[i] = total + bias

    start = SIZE // 2 + left
    streams = [
        (
            conv_buf[0],
            own_cells(shifted, 0, mid, chan),
            [(rows + 1, 0), (1, 2)],
            [0, 1],
            0,
        ),
        (
            conv_buf[1],
            own_cells(shifted, 5, mid, chan),
            [(rows - 5, rows - 4), (rows - 3, rows - 2)],
            [4, 5],
            2,
        ),
        (
            last_buf[...],
            [field[first_row + 3 + h, start : start + SPAN].astype(BF16) for h in range(2)],
            [(rows - 1, rows)],
            [6],
            4,
        ),
    ]
    cells(streams, refs, norm_buf, coarse_in, average)
    load_coarse.wait()
    out_buf[...] = coarse_rows(coarse_in, [(0, 2), (3, 3)], coarse_w, coarse_b)
    count = whole.shape[0]
    low_copy = pltpu.make_async_copy(out_buf.at[:2], whole.at[:2], sems.at[0])
    high_copy = pltpu.make_async_copy(out_buf.at[2:5], whole.at[count - 3 : count], sems.at[1])
    low_copy.start()
    high_copy.start()
    low_copy.wait()
    high_copy.wait()


def local(
    features,
    land_mask,
    dw_weight,
    dw_bias,
    norm_gain,
    norm_shift,
    expand_weight,
    expand_bias,
    project_weight,
    project_bias,
    layer_scale,
    out_gain,
    out_shift,
    coarse_weight,
    coarse_bias,
):
    rows, cols, chan = features.shape
    n_lat = lax.axis_size("lat")
    n_lon = lax.axis_size("lon")
    around = [(i, (i + 1) % n_lon) for i in range(n_lon)]
    back = [(j, i) for i, j in around]
    vmem = pl.BlockSpec(memory_space=pltpu.VMEM)
    side = jax.ShapeDtypeStruct((rows + rows // RIM, RIM, chan), BF16)
    marks = land_mask.astype(BF16)
    to_west, to_east = pl.pallas_call(
        side_kernel,
        out_shape=(side, side),
        grid=(1,),
        in_specs=[
            pl.BlockSpec((rows, 16, chan), lambda i: (0, 0, 0)),
            pl.BlockSpec((rows, 16, chan), lambda i: (0, cols // 16 - 1, 0)),
            vmem,
        ],
        out_specs=(vmem,) * 2,
        compiler_params=pltpu.CompilerParams(vmem_limit_bytes=61000 * 1024),
        name="sides",
    )(features, features, land_mask)
    west = lax.ppermute(to_east, "lon", around)
    east = lax.ppermute(to_west, "lon", back)
    lat = jnp.stack([lax.axis_index("lat"), jnp.int32(n_lat - 1)])
    last = rows // 8 - 1
    scalars = pl.BlockSpec(memory_space=pltpu.SMEM)
    vmem = pl.BlockSpec(memory_space=pltpu.VMEM)
    hbm = pl.BlockSpec(memory_space=pl.ANY)
    band = jax.ShapeDtypeStruct((RIM + 1, SPAN, chan), BF16)
    swap_a, swap_b = pl.pallas_call(
        rim_kernel,
        out_shape=(band, band),
        in_specs=[scalars] + [vmem] * 5,
        out_specs=(vmem, vmem),
        scratch_shapes=[pltpu.VMEM((RIM + 1, SPAN, chan), F32)],
        compiler_params=pltpu.CompilerParams(vmem_limit_bytes=8000 * 1024),
        name="rims",
    )(lat, features[:RIM], features[rows - RIM :], west, east, marks)
    pairs_a = [(i ^ 1, i) for i in range(n_lat)]
    pairs_b = []
    for i in range(n_lat):
        for j in range(n_lon):
            if i == 0:
                to = (0, j)
            elif i == n_lat - 1:
                to = (i, n_lon - 1 - j)
            else:
                to = (((i + 1) ^ 1) - 1, j)
            pairs_b.append((i * n_lon + j, to[0] * n_lon + to[1]))
    rim_b = lax.ppermute(swap_b, ("lat", "lon"), pairs_b)
    rim_a = lax.ppermute(swap_a, "lat", pairs_a)

    hid = expand_weight.shape[1]
    out_count = coarse_weight.shape[3]
    half_cols = cols // 2
    whole_shape = jax.ShapeDtypeStruct((rows // 2, half_cols, out_count), BF16)
    inner_pairs = rows // 2 - GROUP
    norm_gain, norm_shift, expand_bias, project_bias, layer_scale = (
        v[None] for v in (norm_gain, norm_shift, expand_bias, project_bias, layer_scale)
    )
    out_gain, out_shift, coarse_bias, dw_bias = (
        v[None] for v in (out_gain, out_shift, coarse_bias, dw_bias)
    )
    taps_shape = jax.ShapeDtypeStruct((2 * chan, SIZE * 8 * chan), BF16)
    operands = (
        features,
        west,
        east,
        land_mask,
        dw_weight,
        dw_bias,
        norm_gain,
        norm_shift,
        expand_weight,
        expand_bias,
        project_weight,
        project_bias,
        layer_scale,
        out_gain,
        out_shift,
        coarse_bias,
        coarse_weight,
    )
    whole, edges, project, taps = pl.pallas_call(
        inner_kernel,
        out_shape=(
            whole_shape,
            jax.ShapeDtypeStruct((2, half_cols, 8 * chan), BF16),
            jax.ShapeDtypeStruct((hid + chan, chan), BF16),
            taps_shape,
        ),
        in_specs=[vmem] * (len(operands) - 1) + [hbm],
        out_specs=(vmem, vmem, vmem, hbm),
        scratch_shapes=[
            pltpu.VMEM((rows, SPAN + 16, chan), F32),
            pltpu.VMEM((inner_pairs + 3, SPAN, SIZE * 2 * chan), BF16),
            pltpu.VMEM((GROUP, 2, SPAN, chan), F32),
            pltpu.VMEM((inner_pairs, half_cols, 8 * chan), BF16),
            pltpu.VMEM((SPAN, chan), F32),
            pltpu.VMEM((1, chan), F32),
            pltpu.VMEM((2, 2 * SPAN, 2 * chan), F32),
            pltpu.VMEM(taps_shape.shape, BF16),
            pltpu.VMEM(coarse_weight.shape, BF16),
            pltpu.SemaphoreType.DMA((5,)),
        ],
        compiler_params=pltpu.CompilerParams(vmem_limit_bytes=58 * 1024 * 1024),
        cost_estimate=pl.CostEstimate(
            flops=16_000_000_000, bytes_accessed=8_000_000, transcendentals=0
        ),
        name="inner",
    )(*operands)

    operands = (
        lat,
        features,
        features,
        west,
        east,
        rim_a,
        rim_b,
        land_mask,
        dw_weight,
        dw_bias,
        norm_gain,
        norm_shift,
        expand_weight,
        expand_bias,
        project_bias,
        layer_scale,
        out_gain,
        out_shift,
        coarse_bias,
        project,
        taps,
        edges,
        coarse_weight,
        whole,
    )
    specs = [vmem] * (len(operands) - 4) + [hbm] * 4
    specs[0] = scalars
    specs[1] = pl.BlockSpec((8, cols, chan), lambda i: (0, 0, 0))
    specs[2] = pl.BlockSpec((8, cols, chan), lambda i: (last, 0, 0))
    return pl.pallas_call(
        outer_kernel,
        out_shape=whole_shape,
        grid=(1,),
        in_specs=specs,
        out_specs=hbm,
        scratch_shapes=[
            pltpu.VMEM((24, SPAN + 16, chan), F32),
            pltpu.VMEM((10, SPAN, SIZE * 2 * chan), BF16),
            pltpu.VMEM((SPAN, 2 * chan), F32),
            pltpu.VMEM((5, 2, SPAN, chan), F32),
            pltpu.VMEM((7, half_cols, 8 * chan), BF16),
            pltpu.VMEM((SPAN, chan), F32),
            pltpu.VMEM(taps_shape.shape, BF16),
            pltpu.VMEM(coarse_weight.shape, BF16),
            pltpu.VMEM((2, half_cols, 8 * chan), BF16),
            pltpu.VMEM((1, chan), F32),
            pltpu.VMEM((5, half_cols, out_count), BF16),
            pltpu.VMEM((2, 2 * SPAN, 2 * chan), F32),
            pltpu.SemaphoreType.DMA((3,)),
        ],
        input_output_aliases={len(operands) - 1: 0},
        compiler_params=pltpu.CompilerParams(vmem_limit_bytes=64700 * 1024),
        name="outer",
    )(*operands)


def solution(mesh):
    placed = (
        P("lat", "lon", None),
        P("lat", "lon"),
    ) + (P(),) * 13
    return jax.shard_map(
        local, mesh=mesh, in_specs=placed, out_specs=P("lat", "lon", None), check_vma=False
    )
```
